32 devices in a mesh: seq: 8 (over z, x), head: 4 (over y, core).
Axes of the slice: x: 2, y: 2, z: 4, core: 2. Of those that a mesh axis runs over, the one named last changes fastest.
Arguments:
- hidden: bfloat16 [8192, 8192], P('seq'), may hold values from -27 to 27, as said below
- key_value_weight: bfloat16 [8192, 2048], P('seq', 'head'), may hold values from -0.0625 to 0.0625
- down_projection: bfloat16 [2048, 512], P('head'), may hold values from -0.125 to 0.125
- up_projection: bfloat16 [512, 2048], P(None, 'head'), may hold values from -0.25 to 0.25
- positions: int32 [8192], P('seq'), may hold values from 0 to 131071
Outputs:
- grad_down: float32 [512, 2048], P('seq', 'head')
- grad_up: float32 [512, 2048], P('seq', 'head')
- rel_error: float32 [], replicated
The draws below stay inside these ranges and needn't reach their ends.
Inputs may be any that keep to these rules, and one draw needn't show every extreme that they name: `hidden`: real-valued inputs, rows of differing scale.
All inputs are finite; a program needn't handle non-finite values.
Results may differ from the reference program's by a relative error of at most 0.0045.
Values may be sent and summed in bfloat16 or wider, within the bound.
A program may use at most 64 MiB of HBM per device.

```python
import math
import jax
import jax.numpy as jnp
from jax import lax

MODEL_WIDTH = 8192
KEY_VALUE_HEADS = 8
HEAD_SIZE = 128
LATENT_RANK = 512
WINDOW_TOKENS = 8192


def draw_hidden(key, part):
    first_key, second_key = jax.random.split(key, 2)
    row_index = jnp.arange(WINDOW_TOKENS, dtype=jnp.float32)
    row_scale = jnp.exp(jax.random.uniform(second_key, (WINDOW_TOKENS, 1), jnp.float32, jnp.log(0.3), jnp.log(3.0)))
    base = jnp.clip(jax.random.normal(first_key, (WINDOW_TOKENS, MODEL_WIDTH), jnp.float32), -6.0, 6.0)
    ramp = 1.0 + 0.75 * row_index / WINDOW_TOKENS
    return (base * row_scale * ramp[:, None]).astype(jnp.bfloat16)


def plant(array, stream_key, smallest, top_value):
    spot = [jax.random.randint(jax.random.fold_in(stream_key, axis), (), 0, length) for axis, length in enumerate(array.shape)]
    widest = array.shape.index(max(array.shape))
    neighbour = spot[:widest] + [(spot[widest] + 1) % array.shape[widest]] + spot[widest + 1:]
    return array.at[tuple(spot)].set(smallest).at[tuple(neighbour)].set(top_value)


def block_scale(key, extent, cuts, low, largest):
    def one(dim, blocks):
        steps = jax.random.uniform(jax.random.fold_in(jax.random.fold_in(key, 6), dim), (blocks,), jnp.float32, low / len(cuts), largest / len(cuts))
        return jnp.repeat(jnp.exp(steps), extent[dim] // blocks).reshape((-1,) + (1,) * (len(extent) - dim - 1))

    factor_of = one(*cuts[0])
    for cut in cuts[1:]:
        factor_of = factor_of * one(*cut)
    return factor_of


def gaussian(own_key, dims, deviation, limit, cuts=(), kind=jnp.bfloat16):
    array = jax.random.normal(own_key, dims, jnp.float32) * deviation
    if len(cuts) > 0:
        array = block_scale(own_key, dims, cuts, -0.22, 0.18) * array
    return jnp.clip(array, min=-limit, max=limit).astype(kind)


def setup_inputs(seed: int = 0) -> dict:
    arg_keys = jax.random.split(jax.random.key(seed), 6)
    hidden = draw_hidden(jax.random.fold_in(arg_keys[5], 71), 0)
    key_value_weight = gaussian(arg_keys[1], (MODEL_WIDTH, 2 * KEY_VALUE_HEADS * HEAD_SIZE), MODEL_WIDTH ** -0.5, 0.0625, ((0, 8), (1, 4)))
    down_projection = gaussian(arg_keys[2], (2 * KEY_VALUE_HEADS * HEAD_SIZE, LATENT_RANK), (2 * KEY_VALUE_HEADS * HEAD_SIZE) ** -0.5, 0.125, ((0, 4),))
    up_projection = gaussian(arg_keys[3], (LATENT_RANK, 2 * KEY_VALUE_HEADS * HEAD_SIZE), LATENT_RANK ** -0.5, 0.25, ((1, 4),))
    positions = plant(jax.random.randint(arg_keys[4], (WINDOW_TOKENS,), 0, 131072), jax.random.fold_in(arg_keys[4], 1), 0, 131071).astype(jnp.int32)
    return {"hidden": hidden, "key_value_weight": key_value_weight, "down_projection": down_projection, "up_projection": up_projection, "positions": positions}


THETA = 500000.0

def rotate_targets(dense, positions):
    half_dim = HEAD_SIZE // 2
    freqs = jnp.power(jnp.float32(THETA), -(jnp.arange(half_dim, dtype=jnp.float32) * 2.0 / HEAD_SIZE))
    angle = positions.astype(jnp.float32)[:, None] * freqs[None, :]
    cosine = jnp.cos(angle)[:, None, :]
    sine = jnp.sin(angle)[:, None, :]
    shaped = dense.reshape(dense.shape[0], -1, 2, HEAD_SIZE)
    key_part = shaped[:, :, 0, :]
    first = key_part[..., :half_dim]
    second = key_part[..., half_dim:]
    turned = jnp.concatenate([first * cosine - second * sine, second * cosine + first * sine], axis=-1)
    joined = jnp.stack([turned, shaped[:, :, 1, :]], axis=2)
    return joined.reshape(dense.shape[0], -1).astype(jnp.bfloat16)

def reference(hidden, key_value_weight, down_projection, up_projection, positions):
    dense = jnp.dot(hidden, key_value_weight, preferred_element_type=jnp.float32)
    targets = rotate_targets(dense, positions)
    target_wide = targets.astype(jnp.float32)
    energy = jnp.sum(target_wide * target_wide)
    latent = jnp.dot(targets, down_projection, preferred_element_type=jnp.float32).astype(jnp.bfloat16)
    rebuilt = jnp.dot(latent, up_projection, preferred_element_type=jnp.float32)
    residual = target_wide - rebuilt
    rel_error = jnp.sum(residual * residual) / energy
    entry_items = WINDOW_TOKENS * 2 * KEY_VALUE_HEADS * HEAD_SIZE
    factor = -(entry_items / energy) / math.sqrt(WINDOW_TOKENS)
    latent_wide = latent.astype(jnp.float32)
    up_wide = up_projection.astype(jnp.float32)
    grad_up = factor * jnp.dot(latent_wide.T, residual, precision=lax.Precision.HIGHEST, preferred_element_type=jnp.float32)
    d_latent = jnp.dot(residual, up_wide.T, precision=lax.Precision.HIGHEST, preferred_element_type=jnp.float32).astype(jnp.bfloat16)
    grad_down = factor * jnp.dot(d_latent.T, targets, preferred_element_type=jnp.float32)
    return (grad_down, grad_up, rel_error)
```

```python
import functools
import math

import jax
import jax.numpy as jnp
from jax import lax
from jax.experimental import pallas as pl
from jax.experimental.pallas import tpu as pltpu
from jax.sharding import PartitionSpec as P

KEY_VALUE_HEADS = 8
HEAD_SIZE = 128
THETA = 500000.0
MESH = pl.DeviceIdType.MESH
BF16 = jnp.bfloat16
F32 = jnp.float32
LANES = 128


def frequencies():
    half_dim = HEAD_SIZE // 2
    freqs = jnp.power(
        jnp.float32(THETA), -(jnp.arange(half_dim, dtype=jnp.float32) * 2.0 / HEAD_SIZE)
    )
    return jnp.concatenate([freqs, freqs])[None, :]


def cut(depth, B):
    count = max(1, depth // 256)
    if B > 2 or count < 2:
        return tuple(i * (depth // count) for i in range(count + 1)), depth
    late = depth - depth * 11 // 64 // 16 * 16
    bounds = [-(-(late * i // (count - 1)) // 16) * 16 for i in range(count - 1)]
    return tuple(bounds) + (late, depth), late


def kernel(
    A, B, H, bounds, late, entry_items, token_count,
    freq_ref, pos_ref, hidden_ref, weight_ref, down_ref, up_ref,
    gd_ref, gu_ref, rel_ref,
    hid, wbuf, acc, cosine, sine, own_t, all_t, downs, ups, lat_acc, lat, dlat, res, res_o,
    grad, gs1, gr1, gs2, gr2, fin, esum, msum, e0, e1, e2,
    hid_sem, own_sem, mat_sem, send_sem, recv_sem, m_send, m_recv, x_send, x_recv,
    l_send, l_recv, g1_send, g1_recv, g2_send, g2_recv, e_send, e0_recv, e1_recv, e2_recv,
):
    s, h = lax.axis_index("seq"), lax.axis_index("head")
    a, b = s // B, s % B
    y, core = h // 2, h % 2
    other = 1 - core
    sib = y * 2 + other
    N = A * B
    G, _, depth, _ = wbuf.shape
    rows = hid.shape[0]
    tiles, tile = own_t.shape[2:4]
    rank = downs.shape[3]
    cols = ups.shape[2]
    pieces = len(bounds) - 1
    span = depth // pieces

    load = pltpu.make_async_copy(hidden_ref, hid, hid_sem)

    def own_load(g):
        return pltpu.make_async_copy(
            weight_ref.at[:, pl.ds(pl.multiple_of(g * LANES, LANES), LANES)],
            wbuf.at[g, s], own_sem.at[g],
        )

    own_load(0).start()
    own_load(1).start()
    mats = (
        pltpu.make_async_copy(down_ref, downs.at[:, h], mat_sem.at[0]),
        pltpu.make_async_copy(up_ref, ups.at[h], mat_sem.at[1]),
    )

    barrier = pltpu.get_barrier_semaphore()
    for j in range(1, H):
        pl.semaphore_signal(barrier, inc=1, device_id=(s, (h + j) % H), device_id_type=MESH)
    for j in range(1, A):
        pl.semaphore_signal(
            barrier, inc=1, device_id=((a + j) % A * B + b, h), device_id_type=MESH
        )
    for j in range(1, B):
        pl.semaphore_signal(
            barrier, inc=1, device_id=(a * B + (b + j) % B, h), device_id_type=MESH
        )
    load.start()
    for g in range(2, G):
        own_load(g).start()
    for m in mats:
        m.start()
    pl.semaphore_wait(barrier, H - 1 + A - 1 + B - 1)

    def remote(src, dst, ssem, rsem, peer):
        return pltpu.make_async_remote_copy(
            src_ref=src, dst_ref=dst, send_sem=ssem, recv_sem=rsem,
            device_id=peer, device_id_type=MESH,
        )

    ways = (
        (a + 1 < A, s + B),
        (a > 0, s - B),
        (b + 1 < B, s + 1),
        (b > 0, s - 1),
    )

    def part(way, peer, g, o, lo, hi, rsem):
        block = wbuf.at[g, o, pl.ds(lo, hi - lo)]
        return remote(block, block, send_sem.at[way, g, o], rsem, (peer, h))

    def forwards(da, db, g, o, i):
        first = bounds[i] >= late
        conds = (
            (da >= 0) & (first | (db == 0)),
            (da <= 0) & (first | (db == 0)),
            (db >= 0) & ((not first) | (da == 0)),
            (db <= 0) & ((not first) | (da == 0)),
        )
        for way in range(4):
            @pl.when(ways[way][0] & conds[way])
            def _():
                part(
                    way, ways[way][1], g, o, bounds[i], bounds[i + 1], recv_sem.at[g, o, i]
                ).start()

    def own_start(g):
        own_load(g).wait()
        for i in range(pieces):
            forwards(0, 0, g, s, i)

    own_start(0)
    own_start(1)

    def to_head(m, hh):
        if m == 0:
            return remote(down_ref, downs.at[:, h], m_send.at[0, hh], m_recv.at[0, h], (s, hh))
        return remote(up_ref, ups.at[h], m_send.at[1, hh], m_recv.at[1, h], (s, hh))

    def from_head(m, hh):
        if m == 0:
            return remote(down_ref, downs.at[:, hh], m_send.at[0, hh], m_recv.at[0, hh], (s, hh))
        return remote(up_ref, ups.at[hh], m_send.at[1, hh], m_recv.at[1, hh], (s, hh))

    for j in range(1, H):
        to_head(0, (h + j) % H).start()

    lane = lax.broadcasted_iota(jnp.int32, (LANES, LANES), 1)
    low = lane < HEAD_SIZE // 2
    sign = jnp.where(low, -1.0, 1.0)
    pos = pos_ref[...].astype(F32)
    blocks = rows // LANES
    for i in range(blocks // 2):
        k = i + blocks // 2
        p1 = jnp.broadcast_to(pos[i : i + 1], (LANES, LANES)).T
        p2 = jnp.broadcast_to(pos[k : k + 1], (LANES, LANES)).T
        angle = jnp.where(low, p1, p2) * freq_ref[...]
        ca, sa = jnp.cos(angle), jnp.sin(angle)
        cr, sr = pltpu.roll(ca, HEAD_SIZE // 2, 1), pltpu.roll(sa, HEAD_SIZE // 2, 1)
        r1, r2 = slice(i * LANES, (i + 1) * LANES), slice(k * LANES, (k + 1) * LANES)
        cosine[r1] = jnp.where(low, ca, cr)
        cosine[r2] = jnp.where(low, cr, ca)
        sine[r1] = jnp.where(low, sa, sr) * sign
        sine[r2] = jnp.where(low, sr, sa) * sign
    esum[...] = jnp.zeros_like(esum)
    msum[...] = jnp.zeros_like(msum)
    lat_acc[...] = jnp.zeros_like(lat_acc)
    load.wait()

    def product(slot, g, o, q):
        start = pl.multiple_of(o * depth + q * span, span)
        w = wbuf[g, o, q * span : (q + 1) * span]
        step = 512
        for m in range(0, rows, step):
            acc[slot, m : m + step] += jnp.dot(
                hid[m : m + step, pl.ds(start, span)], w, preferred_element_type=F32
            )

    def to_peer(g, r, hh):
        return remote(
            own_t.at[g, hh % 2, r], all_t.at[g, h, r], x_send.at[g, r, hh], x_recv.at[g, r, h],
            (s, hh),
        )

    def from_peer(g, r, hh):
        return remote(
            own_t.at[g, core, r], all_t.at[g, hh, r], x_send.at[g, r, hh], x_recv.at[g, r, hh],
            (s, hh),
        )

    def finish(slot, g):
        is_key = (g % 2) == 0
        for c in range(2):
            for r in range(tiles):
                lo = (c * tiles + r) * tile

                @pl.when(is_key)
                def _():
                    key = acc[slot, lo : lo + tile]
                    turned = key * cosine[lo : lo + tile] + pltpu.roll(
                        key, HEAD_SIZE // 2, 1
                    ) * sine[lo : lo + tile]
                    own_t[g, c, r] = turned.astype(BF16)

                @pl.when(jnp.logical_not(is_key))
                def _():
                    own_t[g, c, r] = acc[slot, lo : lo + tile].astype(BF16)
        for r in range(tiles):
            all_t[g, h, r] = own_t[g, core, r]
        for r in range(tiles):
            for j in range(1, H):
                to_peer(g, r, (h + j) % H).start()

    def latent(g, r):
        for j in range(1, H):
            from_peer(g, r, (h + j) % H).wait_recv()
        x = jnp.concatenate([all_t[g, hh, r] for hh in range(H)], axis=1)
        d = downs[g].reshape(H * LANES, rank)
        lat_acc[r] += jnp.dot(x, d, preferred_element_type=F32)
        wide = x.astype(F32)
        esum[...] += jnp.sum((wide * wide).reshape(tile // 8, 8, H * LANES), axis=0)

    combos = 2 * (2 * B - 1)

    def combo(u, t):
        m = t // 2
        e = (m + 1) // 2
        off = jnp.where(m % 2 == 1, e, -e)
        side = 1 - 2 * (t % 2)
        d = u + 1 - e
        a0, b0 = a + side * d, b + off
        ok = (d >= 0) & (a0 >= 0) & (a0 < A) & (b0 >= 0) & (b0 < B)
        ok = ok & ((side > 0) | (d > 0))
        return ok, a - a0, b - b0, a0 * B + b0

    last_stage = A + B - 3

    def phase(g, carry):
        slot = g % 2
        acc[slot] = jnp.zeros_like(acc[0])
        for q in range(pieces):
            product(slot, g, s, q)

        def stage(u, carry):
            for i in range(pieces):
                def arrive(t, carry):
                    ok, da, db, o = combo(u, t)

                    @pl.when(ok)
                    def _():
                        part(
                            0, s, g, o, bounds[i], bounds[i + 1], recv_sem.at[g, o, i]
                        ).wait_recv()
                        forwards(da, db, g, o, i)
                    return carry
                lax.fori_loop(0, combos, arrive, 0)

                def multiply(t, carry):
                    ok, _, _, o = combo(u, t)

                    @pl.when(ok)
                    def _():
                        product(slot, g, o, i)
                    return carry
                lax.fori_loop(0, combos, multiply, 0)

            @pl.when((u == 0) & (g > 0))
            def _():
                finish(1 - slot, g - 1)

            @pl.when((u == 0) & (g == 1))
            def _():
                for j in range(1, H):
                    to_head(1, (h + j) % H).start()

            @pl.when((u == last_stage) & (g == 1))
            def _():
                mats[0].wait()
                for j in range(1, H):
                    from_head(0, (h + j) % H).wait_recv()

            @pl.when((u == last_stage) & (g > 0))
            def _():
                for r in range(tiles):
                    latent(g - 1, r)
            return carry
        lax.fori_loop(0, last_stage + 1, stage, 0)

        @pl.when(g + 2 < G)
        def _():
            own_start(jnp.minimum(g + 2, G - 1))
        return carry
    lax.fori_loop(0, G, phase, 0)

    def nt(x, w):
        return lax.dot_general(x, w, (((1,), (1,)), ((), ())), preferred_element_type=F32)

    def tn(x, w):
        return lax.dot_general(x, w, (((0,), (0,)), ((), ())), preferred_element_type=F32)

    def to_sib(k, r, c):
        buf = (lat, dlat)[k].at[c, r]
        return remote(buf, buf, l_send.at[k, r], l_recv.at[k, r], (s, sib))

    last = G - 1
    finish(last % 2, last)
    mats[1].wait()
    for j in range(1, H):
        from_head(1, (h + j) % H).wait_recv()

    def columns(ref, *at):
        return jnp.concatenate([ref[(g,) + at] for g in range(G)], axis=1)

    for r in range(tiles):
        latent(last, r)
        narrow = lat_acc[r].astype(BF16)
        lat[core, r] = narrow
        to_sib(0, r, core).start()
        for hh in range(H):
            left = columns(all_t, hh, r).astype(F32) - jnp.dot(
                narrow, ups[hh], preferred_element_type=F32
            )
            res[hh, r] = left.astype(BF16)
            msum[...] += jnp.sum((left * left).reshape(tile // 8, 8, cols), axis=0)

    small = e0.shape[-2:]
    e0[core, 0] = jnp.full(small, jnp.sum(esum[...]), F32)
    e0[core, 1] = jnp.full(small, jnp.sum(msum[...]), F32)

    def level0(c):
        return remote(e0.at[c], e0.at[c], e_send.at[0], e0_recv, (s, sib))

    def level1(bb, slot):
        return remote(e1.at[slot], e1.at[slot], e_send.at[1 + bb], e1_recv.at[slot], (a * B + bb, h))

    def level2(aa, slot):
        return remote(
            e2.at[slot], e2.at[slot], e_send.at[1 + B + aa], e2_recv.at[slot], (aa * B + b, h)
        )

    level0(core).start()

    def first_hop(k, aa, bb, slot):
        return remote(
            gs1.at[k, aa, bb], gr1.at[k, aa, slot], g1_send.at[k, aa, bb], g1_recv.at[k, aa, slot],
            (a * B + bb, h),
        )

    def second_hop(k, aa, slot):
        return remote(
            gs2.at[k, aa], gr2.at[k, slot], g2_send.at[k, aa], g2_recv.at[k, slot],
            (aa * B + b, h),
        )

    def scatter(k, value):
        value = value.reshape(grad.shape[1:])
        grad[k] = value
        gs1[k] = value.astype(BF16)
        for i in range(1, A + 1):
            for j in range(1, B):
                first_hop(k, (a + i) % A, (b + j) % B, b).start()

    def combine(k):
        for i in range(1, A + 1):
            aa = (a + i) % A
            total = grad[k, aa, b]
            for j in range(1, B):
                bb = (b + j) % B
                first_hop(k, aa, bb, bb).wait_recv()
                total += gr1[k, aa, bb].astype(F32)
            if i < A:
                gs2[k, aa] = total.astype(BF16)
                second_hop(k, aa, a).start()
            else:
                fin[k] = total

    for r in range(tiles):
        to_sib(0, r, other).wait_recv()
        left = columns(own_t, other, r).astype(F32) - jnp.dot(
            lat[other, r], ups[h], preferred_element_type=F32
        )
        res_o[r] = left.astype(BF16)
    half = tiles * tile
    scatter(
        0,
        tn(lat[core].reshape(half, rank), res[h].reshape(half, cols))
        + tn(lat[other].reshape(half, rank), res_o[...].reshape(half, cols)),
    )

    for r in range(tiles):
        total = nt(res[0, r], ups[0])
        for hh in range(1, H):
            total += nt(res[hh, r], ups[hh])
        dlat[core, r] = total.astype(BF16)
        to_sib(1, r, core).start()

    level0(other).wait_recv()
    e1[b] = e0[0] + e0[1]
    for j in range(1, B):
        level1((b + j) % B, b).start()

    def targets(c):
        return jnp.concatenate(
            [own_t[g, c].reshape(half, LANES) for g in range(G)], axis=1
        )

    mine = tn(dlat[core].reshape(half, rank), targets(core))
    for r in range(tiles):
        to_sib(1, r, other).wait_recv()
    scatter(1, mine + tn(dlat[other].reshape(half, rank), targets(other)))

    total = None
    for j in range(1, B):
        bb = (b + j) % B
        level1(bb, bb).wait_recv()
    total = e1[0]
    for bb in range(1, B):
        total += e1[bb]
    e2[a] = total
    for j in range(1, A):
        level2((a + j) % A, a).start()

    combine(0)
    combine(1)

    def sends(n, carry):
        g, o = n // N, n % N
        da, db = a - o // B, b - o % B
        zs = (da >= 0, da <= 0)
        xs = (db >= 0, db <= 0)
        for way in range(2):
            @pl.when(ways[way][0] & zs[way] & (db == 0))
            def _():
                part(way, s, g, o, 0, depth, recv_sem.at[g, o, 0]).wait_send()
            if late < depth:
                @pl.when(ways[way][0] & zs[way] & (db != 0))
                def _():
                    part(way, s, g, o, late, depth, recv_sem.at[g, o, 0]).wait_send()
        for way in range(2, 4):
            @pl.when(ways[way][0] & xs[way - 2] & (da == 0))
            def _():
                part(way, s, g, o, 0, depth, recv_sem.at[g, o, 0]).wait_send()

            @pl.when(ways[way][0] & xs[way - 2] & (da != 0))
            def _():
                part(way, s, g, o, 0, late, recv_sem.at[g, o, 0]).wait_send()
        return carry
    lax.fori_loop(0, G * N, sends, 0)
    for j in range(1, H):
        hh = (h + j) % H
        for m in range(2):
            to_head(m, hh).wait_send()
        for r in range(tiles):
            for g in range(G):
                to_peer(g, r, hh).wait_send()
    for k in range(2):
        for r in range(tiles):
            to_sib(k, r, core).wait_send()
        for i in range(1, A + 1):
            for j in range(1, B):
                first_hop(k, (a + i) % A, (b + j) % B, b).wait_send()
    level0(core).wait_send()
    for j in range(1, B):
        level1((b + j) % B, b).wait_send()

    for j in range(1, A):
        aa = (a + j) % A
        level2(aa, aa).wait_recv()
    total = e2[0]
    for aa in range(1, A):
        total += e2[aa]
    whole_energy, whole_misfit = total[0], total[1]
    rel_ref[...] = whole_misfit / whole_energy
    factor = (-(entry_items / whole_energy) / math.sqrt(token_count))[0:1, 0:1]

    for k, out in ((0, gu_ref), (1, gd_ref)):
        total = fin[k]
        for i in range(1, A):
            aa = (a + i) % A
            second_hop(k, aa, aa).wait_recv()
            total += gr2[k, aa].astype(F32)
        out[...] = factor * total
    for k in range(2):
        for i in range(1, A):
            second_hop(k, (a + i) % A, a).wait_send()
    for j in range(1, A):
        level2((a + j) % A, a).wait_send()


def fused(N, H, freqs, positions, hidden, weight, down, up):
    B = 2 if N <= 8 else 8
    A = N // B
    rows, width = hidden.shape
    depth, cols = weight.shape
    rank = down.shape[1]
    G = cols // LANES
    block = rank // N
    tiles = 2
    tile = rows // 2 // tiles
    bounds, late = cut(depth, B)
    pieces = len(bounds) - 1
    token_count = N * rows
    dma = pltpu.SemaphoreType.DMA
    vmem = pl.BlockSpec(memory_space=pltpu.VMEM)
    hbm = pl.BlockSpec(memory_space=pltpu.HBM)
    return pl.pallas_call(
        functools.partial(
            kernel, A, B, H, bounds, late,
            token_count * 2 * KEY_VALUE_HEADS * HEAD_SIZE, token_count,
        ),
        out_shape=(
            jax.ShapeDtypeStruct((block, cols), F32),
            jax.ShapeDtypeStruct((block, cols), F32),
            jax.ShapeDtypeStruct((8, LANES), F32),
        ),
        in_specs=[vmem] * 2 + [hbm] * 4,
        out_specs=(vmem,) * 3,
        scratch_shapes=[
            pltpu.VMEM((rows, width), BF16),
            pltpu.VMEM((G, N, depth, LANES), BF16),
            pltpu.VMEM((2, rows, LANES), F32),
            pltpu.VMEM((rows, LANES), F32),
            pltpu.VMEM((rows, LANES), F32),
            pltpu.VMEM((G, 2, tiles, tile, LANES), BF16),
            pltpu.VMEM((G, H, tiles, tile, LANES), BF16),
            pltpu.VMEM((G, H, LANES, rank), BF16),
            pltpu.VMEM((H, rank, cols), BF16),
            pltpu.VMEM((tiles, tile, rank), F32),
            pltpu.VMEM((2, tiles, tile, rank), BF16),
            pltpu.VMEM((2, tiles, tile, rank), BF16),
            pltpu.VMEM((H, tiles, tile, cols), BF16),
            pltpu.VMEM((tiles, tile, cols), BF16),
            pltpu.VMEM((2, A, B, block, cols), F32),
            pltpu.VMEM((2, A, B, block, cols), BF16),
            pltpu.VMEM((2, A, B, block, cols), BF16),
            pltpu.VMEM((2, A, block, cols), BF16),
            pltpu.VMEM((2, A, block, cols), BF16),
            pltpu.VMEM((2, block, cols), F32),
            pltpu.VMEM((8, H * LANES), F32),
            pltpu.VMEM((8, cols), F32),
            pltpu.VMEM((2, 2, 8, LANES), F32),
            pltpu.VMEM((B, 2, 8, LANES), F32),
            pltpu.VMEM((A, 2, 8, LANES), F32),
            dma,
            dma((G,)),
            dma((2,)),
            dma((4, G, N)),
            dma((G, N, pieces)),
            dma((2, H)),
            dma((2, H)),
            dma((G, tiles, H)),
            dma((G, tiles, H)),
            dma((2, tiles)),
            dma((2, tiles)),
            dma((2, A, B)),
            dma((2, A, B)),
            dma((2, A)),
            dma((2, A)),
            dma((1 + A + B,)),
            dma,
            dma((B,)),
            dma((A,)),
        ],
        compiler_params=pltpu.CompilerParams(
            collective_id=0, has_side_effects=True, vmem_limit_bytes=58 * 2**20
        ),
    )(
        freqs, positions.reshape(rows // LANES, LANES), hidden, weight,
        down.reshape(G, LANES, rank), up,
    )


def solution(mesh):
    N, H = mesh.shape["seq"], mesh.shape["head"]

    def per_device(hidden, key_value_weight, down_projection, up_projection, positions):
        grad_down, grad_up, rel = fused(
            N, H, frequencies(), positions, hidden, key_value_weight, down_projection, up_projection
        )
        return grad_down, grad_up, rel[0, 0]

    return jax.shard_map(
        per_device,
        mesh=mesh,
        in_specs=(P("seq", None), P("seq", "head"), P("head", None), P(None, "head"), P("seq")),
        out_specs=(P("seq", "head"), P("seq", "head"), P()),
        check_vma=False,
    )
```

```python
import functools
import math

import jax
import jax.numpy as jnp
from jax import lax
from jax.experimental import pallas as pl
from jax.experimental.pallas import tpu as pltpu
from jax.sharding import PartitionSpec as P

KEY_VALUE_HEADS = 8
HEAD_SIZE = 128
THETA = 500000.0
MESH = pl.DeviceIdType.MESH
BF16 = jnp.bfloat16
F32 = jnp.float32
LANES = 128


def frequencies():
    half_dim = HEAD_SIZE // 2
    freqs = jnp.power(
        jnp.float32(THETA), -(jnp.arange(half_dim, dtype=jnp.float32) * 2.0 / HEAD_SIZE)
    )
    return jnp.concatenate([freqs, freqs])[None, :]


def cut(depth, B):
    count = max(1, depth // 256)
    if B > 2 or count < 2:
        return tuple(i * (depth // count) for i in range(count + 1)), depth
    late = depth - depth * 11 // 64 // 16 * 16
    bounds = [-(-(late * i // (count - 1)) // 16) * 16 for i in range(count - 1)]
    return tuple(bounds) + (late, depth), late


def kernel(
    A, B, H, bounds, late, entry_items, token_count,
    freq_ref, pos_ref, hidden_ref, weight_ref, down_ref, up_ref,
    gd_ref, gu_ref, rel_ref,
    hid, wbuf, acc, cosine, sine, own_t, all_t, downs, ups, lat_acc, lat, dlat, res, res_o,
    grad, gs1, gr1, gs2, gr2, fin, esum, msum, e0, e1, e2,
    hid_sem, own_sem, mat_sem, send_sem, recv_sem, m_send, m_recv, x_send, x_recv,
    l_send, l_recv, g1_send, g1_recv, g2_send, g2_recv, e_send, e0_recv, e1_recv, e2_recv,
):
    s, h = lax.axis_index("seq"), lax.axis_index("head")
    a, b = s // B, s % B
    y, core = h // 2, h % 2
    other = 1 - core
    sib = y * 2 + other
    N = A * B
    G, _, depth, _ = wbuf.shape
    rows = hid.shape[0]
    tiles, tile = own_t.shape[2:4]
    rank = downs.shape[3]
    cols = ups.shape[2]
    pieces = len(bounds) - 1
    span = depth // pieces

    load = pltpu.make_async_copy(hidden_ref, hid, hid_sem)

    def own_load(g):
        return pltpu.make_async_copy(
            weight_ref.at[:, pl.ds(pl.multiple_of(g * LANES, LANES), LANES)],
            wbuf.at[g, s], own_sem.at[g],
        )

    own_load(0).start()
    own_load(1).start()
    mats = (
        pltpu.make_async_copy(down_ref, downs.at[:, h], mat_sem.at[0]),
        pltpu.make_async_copy(up_ref, ups.at[h], mat_sem.at[1]),
    )

    barrier = pltpu.get_barrier_semaphore()
    for j in range(1, H):
        pl.semaphore_signal(barrier, inc=1, device_id=(s, (h + j) % H), device_id_type=MESH)
    for j in range(1, A):
        pl.semaphore_signal(
            barrier, inc=1, device_id=((a + j) % A * B + b, h), device_id_type=MESH
        )
    for j in range(1, B):
        pl.semaphore_signal(
            barrier, inc=1, device_id=(a * B + (b + j) % B, h), device_id_type=MESH
        )
    load.start()
    for g in range(2, G):
        own_load(g).start()
    for m in mats:
        m.start()
    pl.semaphore_wait(barrier, H - 1 + A - 1 + B - 1)

    def remote(src, dst, ssem, rsem, peer):
        return pltpu.make_async_remote_copy(
            src_ref=src, dst_ref=dst, send_sem=ssem, recv_sem=rsem,
            device_id=peer, device_id_type=MESH,
        )

    ways = (
        (a + 1 < A, s + B),
        (a > 0, s - B),
        (b + 1 < B, s + 1),
        (b > 0, s - 1),
    )

    def part(way, peer, g, o, lo, hi, rsem):
        block = wbuf.at[g, o, pl.ds(lo, hi - lo)]
        return remote(block, block, send_sem.at[way, g, o], rsem, (peer, h))

    def forwards(da, db, g, o, i):
        first = bounds[i] >= late
        conds = (
            (da >= 0) & (first | (db == 0)),
            (da <= 0) & (first | (db == 0)),
            (db >= 0) & ((not first) | (da == 0)),
            (db <= 0) & ((not first) | (da == 0)),
        )
        for way in range(4):
            @pl.when(ways[way][0] & conds[way])
            def _():
                part(
                    way, ways[way][1], g, o, bounds[i], bounds[i + 1], recv_sem.at[g, o, i]
                ).start()

    def own_start(g):
        own_load(g).wait()
        for i in range(pieces):
            forwards(0, 0, g, s, i)

    own_start(0)
    own_start(1)

    def to_head(m, hh):
        if m == 0:
            return remote(down_ref, downs.at[:, h], m_send.at[0, hh], m_recv.at[0, h], (s, hh))
        return remote(up_ref, ups.at[h], m_send.at[1, hh], m_recv.at[1, h], (s, hh))

    def from_head(m, hh):
        if m == 0:
            return remote(down_ref, downs.at[:, hh], m_send.at[0, hh], m_recv.at[0, hh], (s, hh))
        return remote(up_ref, ups.at[hh], m_send.at[1, hh], m_recv.at[1, hh], (s, hh))

    for m in range(2):
        for j in range(1, H):
            to_head(m, (h + j) % H).start()

    lane = lax.broadcasted_iota(jnp.int32, (LANES, LANES), 1)
    low = lane < HEAD_SIZE // 2
    sign = jnp.where(low, -1.0, 1.0)
    pos = pos_ref[...].astype(F32)
    blocks = rows // LANES
    for i in range(blocks // 2):
        k = i + blocks // 2
        p1 = jnp.broadcast_to(pos[i : i + 1], (LANES, LANES)).T
        p2 = jnp.broadcast_to(pos[k : k + 1], (LANES, LANES)).T
        angle = jnp.where(low, p1, p2) * freq_ref[...]
        ca, sa = jnp.cos(angle), jnp.sin(angle)
        cr, sr = pltpu.roll(ca, HEAD_SIZE // 2, 1), pltpu.roll(sa, HEAD_SIZE // 2, 1)
        r1, r2 = slice(i * LANES, (i + 1) * LANES), slice(k * LANES, (k + 1) * LANES)
        cosine[r1] = jnp.where(low, ca, cr)
        cosine[r2] = jnp.where(low, cr, ca)
        sine[r1] = jnp.where(low, sa, sr) * sign
        sine[r2] = jnp.where(low, sr, sa) * sign
    esum[...] = jnp.zeros_like(esum)
    msum[...] = jnp.zeros_like(msum)
    lat_acc[...] = jnp.zeros_like(lat_acc)
    acc[...] = jnp.zeros_like(acc)
    load.wait()

    def product(g, o, q):
        start = pl.multiple_of(o * depth + q * span, span)
        w = wbuf[g, o, q * span : (q + 1) * span]
        step = 512
        for m in range(0, rows, step):
            acc[g, m : m + step] += jnp.dot(
                hid[m : m + step, pl.ds(start, span)], w, preferred_element_type=F32
            )

    def to_peer(g, r, hh):
        return remote(
            own_t.at[g, hh % 2, r], all_t.at[g, h, r], x_send.at[g, r, hh], x_recv.at[g, r, h],
            (s, hh),
        )

    def from_peer(g, r, hh):
        return remote(
            own_t.at[g, core, r], all_t.at[g, hh, r], x_send.at[g, r, hh], x_recv.at[g, r, hh],
            (s, hh),
        )

    def finish(g):
        is_key = (g % 2) == 0
        for c in range(2):
            for r in range(tiles):
                lo = (c * tiles + r) * tile

                @pl.when(is_key)
                def _():
                    key = acc[g, lo : lo + tile]
                    turned = key * cosine[lo : lo + tile] + pltpu.roll(
                        key, HEAD_SIZE // 2, 1
                    ) * sine[lo : lo + tile]
                    own_t[g, c, r] = turned.astype(BF16)

                @pl.when(jnp.logical_not(is_key))
                def _():
                    own_t[g, c, r] = acc[g, lo : lo + tile].astype(BF16)
        for r in range(tiles):
            all_t[g, h, r] = own_t[g, core, r]
        for r in range(tiles):
            for j in range(1, H):
                to_peer(g, r, (h + j) % H).start()

    def latent(g, r):
        for j in range(1, H):
            from_peer(g, r, (h + j) % H).wait_recv()
        x = jnp.concatenate([all_t[g, hh, r] for hh in range(H)], axis=1)
        d = downs[g].reshape(H * LANES, rank)
        lat_acc[r] += jnp.dot(x, d, preferred_element_type=F32)
        wide = x.astype(F32)
        esum[...] += jnp.sum((wide * wide).reshape(tile // 8, 8, H * LANES), axis=0)

    combos = 2 * (2 * B - 1)

    def combo(u, t):
        m = t // 2
        e = (m + 1) // 2
        off = jnp.where(m % 2 == 1, e, -e)
        side = 1 - 2 * (t % 2)
        d = u + 1 - e
        a0, b0 = a + side * d, b + off
        ok = (d >= 0) & (a0 >= 0) & (a0 < A) & (b0 >= 0) & (b0 < B)
        ok = ok & ((side > 0) | (d > 0))
        return ok, a - a0, b - b0, a0 * B + b0

    last_stage = A + B - 3

    def begin(g):
        for q in range(pieces):
            product(g, s, q)

    begin(0)
    begin(1)

    def arrivals(g, u):
        for i in range(pieces):
            def arrive(t, carry):
                ok, da, db, o = combo(u, t)

                @pl.when(ok)
                def _():
                    part(
                        0, s, g, o, bounds[i], bounds[i + 1], recv_sem.at[g, o, i]
                    ).wait_recv()
                    forwards(da, db, g, o, i)
                return carry
            lax.fori_loop(0, combos, arrive, 0)

            def multiply(t, carry):
                ok, _, _, o = combo(u, t)

                @pl.when(ok)
                def _():
                    product(g, o, i)
                return carry
            lax.fori_loop(0, combos, multiply, 0)

    def step(tau, carry):
        def group(g, carry):
            u = tau - g

            @pl.when((u >= 0) & (u <= last_stage))
            def _():
                arrivals(g, u)

            @pl.when((u == last_stage) & (g < G - 1))
            def _():
                finish(g)

            @pl.when((u == last_stage) & (g == 0))
            def _():
                mats[0].wait()
                for j in range(1, H):
                    from_head(0, (h + j) % H).wait_recv()

            @pl.when((u == last_stage) & (g > 0) & (g < G - 1))
            def _():
                for r in range(tiles):
                    latent(jnp.maximum(g - 1, 0), r)

            @pl.when(u == -2)
            def _():
                own_start(g)
                begin(g)
            return carry
        return lax.fori_loop(0, G, group, carry)
    lax.fori_loop(0, last_stage + G, step, 0)

    def nt(x, w):
        return lax.dot_general(x, w, (((1,), (1,)), ((), ())), preferred_element_type=F32)

    def tn(x, w):
        return lax.dot_general(x, w, (((0,), (0,)), ((), ())), preferred_element_type=F32)

    def to_sib(k, r, c):
        buf = (lat, dlat)[k].at[c, r]
        return remote(buf, buf, l_send.at[k, r], l_recv.at[k, r], (s, sib))

    last = G - 1
    finish(last)
    for r in range(tiles):
        latent(last - 1, r)
    mats[1].wait()
    for j in range(1, H):
        from_head(1, (h + j) % H).wait_recv()

    def columns(ref, *at):
        return jnp.concatenate([ref[(g,) + at] for g in range(G)], axis=1)

    for r in range(tiles):
        latent(last, r)
        narrow = lat_acc[r].astype(BF16)
        lat[core, r] = narrow
        to_sib(0, r, core).start()
        for hh in range(H):
            left = columns(all_t, hh, r).astype(F32) - jnp.dot(
                narrow, ups[hh], preferred_element_type=F32
            )
            res[hh, r] = left.astype(BF16)
            msum[...] += jnp.sum((left * left).reshape(tile // 8, 8, cols), axis=0)

    small = e0.shape[-2:]
    e0[core, 0] = jnp.full(small, jnp.sum(esum[...]), F32)
    e0[core, 1] = jnp.full(small, jnp.sum(msum[...]), F32)

    def level0(c):
        return remote(e0.at[c], e0.at[c], e_send.at[0], e0_recv, (s, sib))

    def level1(bb, slot):
        return remote(e1.at[slot], e1.at[slot], e_send.at[1 + bb], e1_recv.at[slot], (a * B + bb, h))

    def level2(aa, slot):
        return remote(
            e2.at[slot], e2.at[slot], e_send.at[1 + B + aa], e2_recv.at[slot], (aa * B + b, h)
        )

    level0(core).start()

    def first_hop(k, aa, bb, slot):
        return remote(
            gs1.at[k, aa, bb], gr1.at[k, aa, slot], g1_send.at[k, aa, bb], g1_recv.at[k, aa, slot],
            (a * B + bb, h),
        )

    def second_hop(k, aa, slot):
        return remote(
            gs2.at[k, aa], gr2.at[k, slot], g2_send.at[k, aa], g2_recv.at[k, slot],
            (aa * B + b, h),
        )

    def scatter(k, value):
        value = value.reshape(grad.shape[1:])
        grad[k] = value
        gs1[k] = value.astype(BF16)
        for i in range(1, A + 1):
            for j in range(1, B):
                first_hop(k, (a + i) % A, (b + j) % B, b).start()

    def combine(k):
        for i in range(1, A + 1):
            aa = (a + i) % A
            total = grad[k, aa, b]
            for j in range(1, B):
                bb = (b + j) % B
                first_hop(k, aa, bb, bb).wait_recv()
                total += gr1[k, aa, bb].astype(F32)
            if i < A:
                gs2[k, aa] = total.astype(BF16)
                second_hop(k, aa, a).start()
            else:
                fin[k] = total

    for r in range(tiles):
        to_sib(0, r, other).wait_recv()
        left = columns(own_t, other, r).astype(F32) - jnp.dot(
            lat[other, r], ups[h], preferred_element_type=F32
        )
        res_o[r] = left.astype(BF16)
    half = tiles * tile
    scatter(
        0,
        tn(lat[core].reshape(half, rank), res[h].reshape(half, cols))
        + tn(lat[other].reshape(half, rank), res_o[...].reshape(half, cols)),
    )

    for r in range(tiles):
        total = nt(res[0, r], ups[0])
        for hh in range(1, H):
            total += nt(res[hh, r], ups[hh])
        dlat[core, r] = total.astype(BF16)
        to_sib(1, r, core).start()

    level0(other).wait_recv()
    e1[b] = e0[0] + e0[1]
    for j in range(1, B):
        level1((b + j) % B, b).start()

    def targets(c):
        return jnp.concatenate(
            [own_t[g, c].reshape(half, LANES) for g in range(G)], axis=1
        )

    mine = tn(dlat[core].reshape(half, rank), targets(core))
    for r in range(tiles):
        to_sib(1, r, other).wait_recv()
    scatter(1, mine + tn(dlat[other].reshape(half, rank), targets(other)))

    total = None
    for j in range(1, B):
        bb = (b + j) % B
        level1(bb, bb).wait_recv()
    total = e1[0]
    for bb in range(1, B):
        total += e1[bb]
    e2[a] = total
    for j in range(1, A):
        level2((a + j) % A, a).start()

    combine(0)
    combine(1)

    def sends(n, carry):
        g, o = n // N, n % N
        da, db = a - o // B, b - o % B
        zs = (da >= 0, da <= 0)
        xs = (db >= 0, db <= 0)
        for way in range(2):
            @pl.when(ways[way][0] & zs[way] & (db == 0))
            def _():
                part(way, s, g, o, 0, depth, recv_sem.at[g, o, 0]).wait_send()
            if late < depth:
                @pl.when(ways[way][0] & zs[way] & (db != 0))
                def _():
                    part(way, s, g, o, late, depth, recv_sem.at[g, o, 0]).wait_send()
        for way in range(2, 4):
            @pl.when(ways[way][0] & xs[way - 2] & (da == 0))
            def _():
                part(way, s, g, o, 0, depth, recv_sem.at[g, o, 0]).wait_send()

            @pl.when(ways[way][0] & xs[way - 2] & (da != 0))
            def _():
                part(way, s, g, o, 0, late, recv_sem.at[g, o, 0]).wait_send()
        return carry
    lax.fori_loop(0, G * N, sends, 0)
    for j in range(1, H):
        hh = (h + j) % H
        for m in range(2):
            to_head(m, hh).wait_send()
        for r in range(tiles):
            for g in range(G):
                to_peer(g, r, hh).wait_send()
    for k in range(2):
        for r in range(tiles):
            to_sib(k, r, core).wait_send()
        for i in range(1, A + 1):
            for j in range(1, B):
                first_hop(k, (a + i) % A, (b + j) % B, b).wait_send()
    level0(core).wait_send()
    for j in range(1, B):
        level1((b + j) % B, b).wait_send()

    for j in range(1, A):
        aa = (a + j) % A
        level2(aa, aa).wait_recv()
    total = e2[0]
    for aa in range(1, A):
        total += e2[aa]
    whole_energy, whole_misfit = total[0], total[1]
    rel_ref[...] = whole_misfit / whole_energy
    factor = (-(entry_items / whole_energy) / math.sqrt(token_count))[0:1, 0:1]

    for k, out in ((0, gu_ref), (1, gd_ref)):
        total = fin[k]
        for i in range(1, A):
            aa = (a + i) % A
            second_hop(k, aa, aa).wait_recv()
            total += gr2[k, aa].astype(F32)
        out[...] = factor * total
    for k in range(2):
        for i in range(1, A):
            second_hop(k, (a + i) % A, a).wait_send()
    for j in range(1, A):
        level2((a + j) % A, a).wait_send()


def fused(N, H, freqs, positions, hidden, weight, down, up):
    B = 2 if N <= 8 else 8
    A = N // B
    rows, width = hidden.shape
    depth, cols = weight.shape
    rank = down.shape[1]
    G = cols // LANES
    block = rank // N
    tiles = 2
    tile = rows // 2 // tiles
    bounds, late = cut(depth, B)
    pieces = len(bounds) - 1
    token_count = N * rows
    dma = pltpu.SemaphoreType.DMA
    vmem = pl.BlockSpec(memory_space=pltpu.VMEM)
    hbm = pl.BlockSpec(memory_space=pltpu.HBM)
    return pl.pallas_call(
        functools.partial(
            kernel, A, B, H, bounds, late,
            token_count * 2 * KEY_VALUE_HEADS * HEAD_SIZE, token_count,
        ),
        out_shape=(
            jax.ShapeDtypeStruct((block, cols), F32),
            jax.ShapeDtypeStruct((block, cols), F32),
            jax.ShapeDtypeStruct((8, LANES), F32),
        ),
        in_specs=[vmem] * 2 + [hbm] * 4,
        out_specs=(vmem,) * 3,
        scratch_shapes=[
            pltpu.VMEM((rows, width), BF16),
            pltpu.VMEM((G, N, depth, LANES), BF16),
            pltpu.VMEM((G, rows, LANES), F32),
            pltpu.VMEM((rows, LANES), F32),
            pltpu.VMEM((rows, LANES), F32),
            pltpu.VMEM((G, 2, tiles, tile, LANES), BF16),
            pltpu.VMEM((G, H, tiles, tile, LANES), BF16),
            pltpu.VMEM((G, H, LANES, rank), BF16),
            pltpu.VMEM((H, rank, cols), BF16),
            pltpu.VMEM((tiles, tile, rank), F32),
            pltpu.VMEM((2, tiles, tile, rank), BF16),
            pltpu.VMEM((2, tiles, tile, rank), BF16),
            pltpu.VMEM((H, tiles, tile, cols), BF16),
            pltpu.VMEM((tiles, tile, cols), BF16),
            pltpu.VMEM((2, A, B, block, cols), F32),
            pltpu.VMEM((2, A, B, block, cols), BF16),
            pltpu.VMEM((2, A, B, block, cols), BF16),
            pltpu.VMEM((2, A, block, cols), BF16),
            pltpu.VMEM((2, A, block, cols), BF16),
            pltpu.VMEM((2, block, cols), F32),
            pltpu.VMEM((8, H * LANES), F32),
            pltpu.VMEM((8, cols), F32),
            pltpu.VMEM((2, 2, 8, LANES), F32),
            pltpu.VMEM((B, 2, 8, LANES), F32),
            pltpu.VMEM((A, 2, 8, LANES), F32),
            dma,
            dma((G,)),
            dma((2,)),
            dma((4, G, N)),
            dma((G, N, pieces)),
            dma((2, H)),
            dma((2, H)),
            dma((G, tiles, H)),
            dma((G, tiles, H)),
            dma((2, tiles)),
            dma((2, tiles)),
            dma((2, A, B)),
            dma((2, A, B)),
            dma((2, A)),
            dma((2, A)),
            dma((1 + A + B,)),
            dma,
            dma((B,)),
            dma((A,)),
        ],
        compiler_params=pltpu.CompilerParams(
            collective_id=0, has_side_effects=True, vmem_limit_bytes=50 * 2**20
        ),
    )(
        freqs, positions.reshape(rows // LANES, LANES), hidden, weight,
        down.reshape(G, LANES, rank), up,
    )


def solution(mesh):
    N, H = mesh.shape["seq"], mesh.shape["head"]

    def per_device(hidden, key_value_weight, down_projection, up_projection, positions):
        grad_down, grad_up, rel = fused(
            N, H, frequencies(), positions, hidden, key_value_weight, down_projection, up_projection
        )
        return grad_down, grad_up, rel[0, 0]

    return jax.shard_map(
        per_device,
        mesh=mesh,
        in_specs=(P("seq", None), P("seq", "head"), P("head", None), P(None, "head"), P("seq")),
        out_specs=(P("seq", "head"), P("seq", "head"), P()),
        check_vma=False,
    )
```

```python
import functools
import math

import jax
import jax.numpy as jnp
from jax import lax
from jax.experimental import pallas as pl
from jax.experimental.pallas import tpu as pltpu
from jax.sharding import PartitionSpec as P

KEY_VALUE_HEADS = 8
HEAD_SIZE = 128
THETA = 500000.0
MESH = pl.DeviceIdType.MESH
BF16 = jnp.bfloat16
F32 = jnp.float32
LANES = 128
PIECES = 2


def frequencies():
    half_dim = HEAD_SIZE // 2
    freqs = jnp.power(
        jnp.float32(THETA), -(jnp.arange(half_dim, dtype=jnp.float32) * 2.0 / HEAD_SIZE)
    )
    return jnp.concatenate([freqs, freqs])[None, :]


def cut(depth, B):
    count = PIECES
    if B > 2 or depth < 512:
        return (0, depth), depth
    late = depth - depth * 11 // 64 // 16 * 16
    bounds = [-(-(late * i // (count - 1)) // 16) * 16 for i in range(count - 1)]
    return tuple(bounds) + (late, depth), late


def kernel(
    A, B, H, bounds, late, entry_items, token_count,
    freq_ref, pos_ref, hidden_ref, weight_ref, down_ref, up_ref,
    gd_ref, gu_ref, rel_ref,
    hid, wbuf, acc, cosine, sine, own_t, all_t, downs, ups, lat_acc, lat, dlat, res, res_o,
    grad, gs1, gr1, gs2, gr2, fin, esum, msum, e0, e1, e2,
    hid_sem, own_sem, mat_sem, send_sem, recv_sem, m_send, m_recv, x_send, x_recv,
    l_send, l_recv, g1_send, g1_recv, g2_send, g2_recv, e_send, e0_recv, e1_recv, e2_recv,
):
    s, h = lax.axis_index("seq"), lax.axis_index("head")
    a, b = s // B, s % B
    y, core = h // 2, h % 2
    other = 1 - core
    sib = y * 2 + other
    N = A * B
    G, _, depth, _ = wbuf.shape
    rows = hid.shape[0]
    tiles, tile = own_t.shape[2:4]
    rank = downs.shape[3]
    cols = ups.shape[2]
    pieces = len(bounds) - 1
    spans = [bound // 256 * 256 for bound in bounds[:-1]] + [depth]

    load = pltpu.make_async_copy(hidden_ref, hid, hid_sem)

    def own_load(g):
        return pltpu.make_async_copy(
            weight_ref.at[:, pl.ds(pl.multiple_of(g * LANES, LANES), LANES)],
            wbuf.at[g, s], own_sem.at[g],
        )

    own_load(0).start()
    own_load(1).start()
    mats = (
        pltpu.make_async_copy(down_ref, downs.at[:, h], mat_sem.at[0]),
        pltpu.make_async_copy(up_ref, ups.at[h], mat_sem.at[1]),
    )

    barrier = pltpu.get_barrier_semaphore()
    for j in range(1, H):
        pl.semaphore_signal(barrier, inc=1, device_id=(s, (h + j) % H), device_id_type=MESH)
    for j in range(1, A):
        pl.semaphore_signal(
            barrier, inc=1, device_id=((a + j) % A * B + b, h), device_id_type=MESH
        )
    for j in range(1, B):
        pl.semaphore_signal(
            barrier, inc=1, device_id=(a * B + (b + j) % B, h), device_id_type=MESH
        )
    load.start()
    for g in range(2, G):
        own_load(g).start()
    for m in mats:
        m.start()
    pl.semaphore_wait(barrier, H - 1 + A - 1 + B - 1)

    def remote(src, dst, ssem, rsem, peer):
        return pltpu.make_async_remote_copy(
            src_ref=src, dst_ref=dst, send_sem=ssem, recv_sem=rsem,
            device_id=peer, device_id_type=MESH,
        )

    ways = (
        (a + 1 < A, s + B),
        (a > 0, s - B),
        (b + 1 < B, s + 1),
        (b > 0, s - 1),
    )

    def part(way, peer, g, o, lo, hi, rsem):
        block = wbuf.at[g, o, pl.ds(lo, hi - lo)]
        return remote(block, block, send_sem.at[way, g, o], rsem, (peer, h))

    def forwards(da, db, g, o, i):
        first = bounds[i] >= late
        conds = (
            (da >= 0) & (first | (db == 0)),
            (da <= 0) & (first | (db == 0)),
            (db >= 0) & ((not first) | (da == 0)),
            (db <= 0) & ((not first) | (da == 0)),
        )
        for way in range(4):
            @pl.when(ways[way][0] & conds[way])
            def _():
                part(
                    way, ways[way][1], g, o, bounds[i], bounds[i + 1], recv_sem.at[g, o, i]
                ).start()

    def own_start(g):
        own_load(g).wait()
        for i in range(pieces):
            forwards(0, 0, g, s, i)

    own_start(0)
    own_start(1)

    def to_head(m, hh):
        if m == 0:
            return remote(down_ref, downs.at[:, h], m_send.at[0, hh], m_recv.at[0, h], (s, hh))
        return remote(up_ref, ups.at[h], m_send.at[1, hh], m_recv.at[1, h], (s, hh))

    def from_head(m, hh):
        if m == 0:
            return remote(down_ref, downs.at[:, hh], m_send.at[0, hh], m_recv.at[0, hh], (s, hh))
        return remote(up_ref, ups.at[hh], m_send.at[1, hh], m_recv.at[1, hh], (s, hh))

    for m in range(2):
        for j in range(1, H):
            to_head(m, (h + j) % H).start()

    lane = lax.broadcasted_iota(jnp.int32, (LANES, LANES), 1)
    low = lane < HEAD_SIZE // 2
    sign = jnp.where(low, -1.0, 1.0)
    pos = pos_ref[...].astype(F32)
    blocks = rows // LANES
    for i in range(blocks // 2):
        k = i + blocks // 2
        p1 = jnp.broadcast_to(pos[i : i + 1], (LANES, LANES)).T
        p2 = jnp.broadcast_to(pos[k : k + 1], (LANES, LANES)).T
        angle = jnp.where(low, p1, p2) * freq_ref[...]
        ca, sa = jnp.cos(angle), jnp.sin(angle)
        cr, sr = pltpu.roll(ca, HEAD_SIZE // 2, 1), pltpu.roll(sa, HEAD_SIZE // 2, 1)
        r1, r2 = slice(i * LANES, (i + 1) * LANES), slice(k * LANES, (k + 1) * LANES)
        cosine[r1] = jnp.where(low, ca, cr)
        cosine[r2] = jnp.where(low, cr, ca)
        sine[r1] = jnp.where(low, sa, sr) * sign
        sine[r2] = jnp.where(low, sr, sa) * sign
    esum[...] = jnp.zeros_like(esum)
    msum[...] = jnp.zeros_like(msum)
    lat_acc[...] = jnp.zeros_like(lat_acc)
    acc[...] = jnp.zeros_like(acc)
    load.wait()

    def product(g, o, q):
        lo, span = spans[q], spans[q + 1] - spans[q]
        start = pl.multiple_of(o * depth + lo, min(span, 256))
        w = wbuf[g, o, lo : lo + span]
        step = 512
        for m in range(0, rows, step):
            acc[g, m : m + step] += jnp.dot(
                hid[m : m + step, pl.ds(start, span)], w, preferred_element_type=F32
            )

    def to_peer(g, r, hh):
        return remote(
            own_t.at[g, hh % 2, r], all_t.at[g, h, r], x_send.at[g, r, hh], x_recv.at[g, r, h],
            (s, hh),
        )

    def from_peer(g, r, hh):
        return remote(
            own_t.at[g, core, r], all_t.at[g, hh, r], x_send.at[g, r, hh], x_recv.at[g, r, hh],
            (s, hh),
        )

    def finish(g):
        is_key = (g % 2) == 0
        for c in range(2):
            for r in range(tiles):
                lo = (c * tiles + r) * tile

                @pl.when(is_key)
                def _():
                    key = acc[g, lo : lo + tile]
                    turned = key * cosine[lo : lo + tile] + pltpu.roll(
                        key, HEAD_SIZE // 2, 1
                    ) * sine[lo : lo + tile]
                    own_t[g, c, r] = turned.astype(BF16)

                @pl.when(jnp.logical_not(is_key))
                def _():
                    own_t[g, c, r] = acc[g, lo : lo + tile].astype(BF16)
        for r in range(tiles):
            all_t[g, h, r] = own_t[g, core, r]
        for r in range(tiles):
            for j in range(1, H):
                to_peer(g, r, (h + j) % H).start()

    def latent(g, r):
        for j in range(1, H):
            from_peer(g, r, (h + j) % H).wait_recv()
        x = jnp.concatenate([all_t[g, hh, r] for hh in range(H)], axis=1)
        d = downs[g].reshape(H * LANES, rank)
        lat_acc[r] += jnp.dot(x, d, preferred_element_type=F32)
        wide = x.astype(F32)
        esum[...] += jnp.sum((wide * wide).reshape(tile // 8, 8, H * LANES), axis=0)

    combos = 2 * (2 * B - 1)

    def combo(u, t):
        m = t // 2
        e = (m + 1) // 2
        off = e if m % 2 == 1 else -e
        side = 1 - 2 * (t % 2)
        d = u + 1 - e
        a0, b0 = a + side * d, b + off
        ok = (d >= 0) & (a0 >= 0) & (a0 < A) & (b0 >= 0) & (b0 < B)
        ok = ok & ((d > 0) | (side > 0))
        return ok, a - a0, b - b0, a0 * B + b0

    last_stage = A + B - 3

    def begin(g):
        for q in range(pieces):
            product(g, s, q)

    begin(0)
    begin(1)

    def arrivals(g, u):
        for i in range(pieces):
            def arrive(t, carry):
                ok, da, db, o = combo(u, t)

                @pl.when(ok)
                def _():
                    part(
                        0, s, g, o, bounds[i], bounds[i + 1], recv_sem.at[g, o, i]
                    ).wait_recv()
                    forwards(da, db, g, o, i)
                return carry
            [arrive(t, 0) for t in range(combos)]

            def multiply(t, carry):
                ok, _, _, o = combo(u, t)

                @pl.when(ok)
                def _():
                    product(g, o, i)
                return carry
            [multiply(t, 0) for t in range(combos)]

    def step(tau, carry):
        def group(g, carry):
            u = tau - g

            @pl.when((u >= 0) & (u <= last_stage))
            def _():
                arrivals(g, u)

            @pl.when((u == last_stage) & (g < G - 1))
            def _():
                finish(g)

            @pl.when((u == last_stage) & (g == 0))
            def _():
                mats[0].wait()
                for j in range(1, H):
                    from_head(0, (h + j) % H).wait_recv()

            @pl.when((u == last_stage) & (g > 0) & (g < G - 1))
            def _():
                for r in range(tiles):
                    latent(jnp.maximum(g - 1, 0), r)

            @pl.when(u == -2)
            def _():
                own_start(g)
                begin(g)
            return carry
        return lax.fori_loop(0, G, group, carry)
    lax.fori_loop(0, last_stage + G, step, 0)

    def nt(x, w):
        return lax.dot_general(x, w, (((1,), (1,)), ((), ())), preferred_element_type=F32)

    def tn(x, w):
        return lax.dot_general(x, w, (((0,), (0,)), ((), ())), preferred_element_type=F32)

    def to_sib(k, r, c):
        buf = (lat, dlat)[k].at[c, r]
        return remote(buf, buf, l_send.at[k, r], l_recv.at[k, r], (s, sib))

    last = G - 1
    finish(last)
    for r in range(tiles):
        latent(last - 1, r)
    mats[1].wait()
    for j in range(1, H):
        from_head(1, (h + j) % H).wait_recv()

    def columns(ref, *at):
        return jnp.concatenate([ref[(g,) + at] for g in range(G)], axis=1)

    for r in range(tiles):
        latent(last, r)
        narrow = lat_acc[r].astype(BF16)
        lat[core, r] = narrow
        to_sib(0, r, core).start()
        for hh in range(H):
            left = columns(all_t, hh, r).astype(F32) - jnp.dot(
                narrow, ups[hh], preferred_element_type=F32
            )
            res[hh, r] = left.astype(BF16)
            msum[...] += jnp.sum((left * left).reshape(tile // 8, 8, cols), axis=0)

    small = e0.shape[-2:]
    e0[core, 0] = jnp.full(small, jnp.sum(esum[...]), F32)
    e0[core, 1] = jnp.full(small, jnp.sum(msum[...]), F32)

    def level0(c):
        return remote(e0.at[c], e0.at[c], e_send.at[0], e0_recv, (s, sib))

    def level1(bb, slot):
        return remote(e1.at[slot], e1.at[slot], e_send.at[1 + bb], e1_recv.at[slot], (a * B + bb, h))

    def level2(aa, slot):
        return remote(
            e2.at[slot], e2.at[slot], e_send.at[1 + B + aa], e2_recv.at[slot], (aa * B + b, h)
        )

    level0(core).start()

    def first_hop(k, aa, bb, slot):
        return remote(
            gs1.at[k, aa, bb], gr1.at[k, aa, slot], g1_send.at[k, aa, bb], g1_recv.at[k, aa, slot],
            (a * B + bb, h),
        )

    def second_hop(k, aa, slot):
        return remote(
            gs2.at[k, aa], gr2.at[k, slot], g2_send.at[k, aa], g2_recv.at[k, slot],
            (aa * B + b, h),
        )

    def scatter(k, value):
        value = value.reshape(grad.shape[1:])
        grad[k] = value
        gs1[k] = value.astype(BF16)
        for i in range(1, A + 1):
            for j in range(1, B):
                first_hop(k, (a + i) % A, (b + j) % B, b).start()

    def combine(k):
        for i in range(1, A + 1):
            aa = (a + i) % A
            total = grad[k, aa, b]
            for j in range(1, B):
                bb = (b + j) % B
                first_hop(k, aa, bb, bb).wait_recv()
                total += gr1[k, aa, bb].astype(F32)
            if i < A:
                gs2[k, aa] = total.astype(BF16)
                second_hop(k, aa, a).start()
            else:
                fin[k] = total

    for r in range(tiles):
        to_sib(0, r, other).wait_recv()
        left = columns(own_t, other, r).astype(F32) - jnp.dot(
            lat[other, r], ups[h], preferred_element_type=F32
        )
        res_o[r] = left.astype(BF16)
    half = tiles * tile
    scatter(
        0,
        tn(lat[core].reshape(half, rank), res[h].reshape(half, cols))
        + tn(lat[other].reshape(half, rank), res_o[...].reshape(half, cols)),
    )

    for r in range(tiles):
        total = nt(res[0, r], ups[0])
        for hh in range(1, H):
            total += nt(res[hh, r], ups[hh])
        dlat[core, r] = total.astype(BF16)
        to_sib(1, r, core).start()

    level0(other).wait_recv()
    e1[b] = e0[0] + e0[1]
    for j in range(1, B):
        level1((b + j) % B, b).start()

    def targets(c):
        return jnp.concatenate(
            [own_t[g, c].reshape(half, LANES) for g in range(G)], axis=1
        )

    mine = tn(dlat[core].reshape(half, rank), targets(core))
    for r in range(tiles):
        to_sib(1, r, other).wait_recv()
    scatter(1, mine + tn(dlat[other].reshape(half, rank), targets(other)))

    total = None
    for j in range(1, B):
        bb = (b + j) % B
        level1(bb, bb).wait_recv()
    total = e1[0]
    for bb in range(1, B):
        total += e1[bb]
    e2[a] = total
    for j in range(1, A):
        level2((a + j) % A, a).start()

    combine(0)
    combine(1)

    def sends(n, carry):
        g, o = n // N, n % N
        da, db = a - o // B, b - o % B
        zs = (da >= 0, da <= 0)
        xs = (db >= 0, db <= 0)
        for way in range(2):
            @pl.when(ways[way][0] & zs[way] & (db == 0))
            def _():
                part(way, s, g, o, 0, depth, recv_sem.at[g, o, 0]).wait_send()
            if late < depth:
                @pl.when(ways[way][0] & zs[way] & (db != 0))
                def _():
                    part(way, s, g, o, late, depth, recv_sem.at[g, o, 0]).wait_send()
        for way in range(2, 4):
            @pl.when(ways[way][0] & xs[way - 2] & (da == 0))
            def _():
                part(way, s, g, o, 0, depth, recv_sem.at[g, o, 0]).wait_send()

            @pl.when(ways[way][0] & xs[way - 2] & (da != 0))
            def _():
                part(way, s, g, o, 0, late, recv_sem.at[g, o, 0]).wait_send()
        return carry
    lax.fori_loop(0, G * N, sends, 0)
    for j in range(1, H):
        hh = (h + j) % H
        for m in range(2):
            to_head(m, hh).wait_send()
        for r in range(tiles):
            for g in range(G):
                to_peer(g, r, hh).wait_send()
    for k in range(2):
        for r in range(tiles):
            to_sib(k, r, core).wait_send()
        for i in range(1, A + 1):
            for j in range(1, B):
                first_hop(k, (a + i) % A, (b + j) % B, b).wait_send()
    level0(core).wait_send()
    for j in range(1, B):
        level1((b + j) % B, b).wait_send()

    for j in range(1, A):
        aa = (a + j) % A
        level2(aa, aa).wait_recv()
    total = e2[0]
    for aa in range(1, A):
        total += e2[aa]
    whole_energy, whole_misfit = total[0], total[1]
    rel_ref[...] = whole_misfit / whole_energy
    factor = (-(entry_items / whole_energy) / math.sqrt(token_count))[0:1, 0:1]

    for k, out in ((0, gu_ref), (1, gd_ref)):
        total = fin[k]
        for i in range(1, A):
            aa = (a + i) % A
            second_hop(k, aa, aa).wait_recv()
            total += gr2[k, aa].astype(F32)
        out[...] = factor * total
    for k in range(2):
        for i in range(1, A):
            second_hop(k, (a + i) % A, a).wait_send()
    for j in range(1, A):
        level2((a + j) % A, a).wait_send()


def fused(N, H, freqs, positions, hidden, weight, down, up):
    B = 2 if N <= 8 else 8
    A = N // B
    rows, width = hidden.shape
    depth, cols = weight.shape
    rank = down.shape[1]
    G = cols // LANES
    block = rank // N
    tiles = 2
    tile = rows // 2 // tiles
    bounds, late = cut(depth, B)
    pieces = len(bounds) - 1
    token_count = N * rows
    dma = pltpu.SemaphoreType.DMA
    vmem = pl.BlockSpec(memory_space=pltpu.VMEM)
    hbm = pl.BlockSpec(memory_space=pltpu.HBM)
    return pl.pallas_call(
        functools.partial(
            kernel, A, B, H, bounds, late,
            token_count * 2 * KEY_VALUE_HEADS * HEAD_SIZE, token_count,
        ),
        out_shape=(
            jax.ShapeDtypeStruct((block, cols), F32),
            jax.ShapeDtypeStruct((block, cols), F32),
            jax.ShapeDtypeStruct((8, LANES), F32),
        ),
        in_specs=[vmem] * 2 + [hbm] * 4,
        out_specs=(vmem,) * 3,
        scratch_shapes=[
            pltpu.VMEM((rows, width), BF16),
            pltpu.VMEM((G, N, depth, LANES), BF16),
            pltpu.VMEM((G, rows, LANES), F32),
            pltpu.VMEM((rows, LANES), F32),
            pltpu.VMEM((rows, LANES), F32),
            pltpu.VMEM((G, 2, tiles, tile, LANES), BF16),
            pltpu.VMEM((G, H, tiles, tile, LANES), BF16),
            pltpu.VMEM((G, H, LANES, rank), BF16),
            pltpu.VMEM((H, rank, cols), BF16),
            pltpu.VMEM((tiles, tile, rank), F32),
            pltpu.VMEM((2, tiles, tile, rank), BF16),
            pltpu.VMEM((2, tiles, tile, rank), BF16),
            pltpu.VMEM((H, tiles, tile, cols), BF16),
            pltpu.VMEM((tiles, tile, cols), BF16),
            pltpu.VMEM((2, A, B, block, cols), F32),
            pltpu.VMEM((2, A, B, block, cols), BF16),
            pltpu.VMEM((2, A, B, block, cols), BF16),
            pltpu.VMEM((2, A, block, cols), BF16),
            pltpu.VMEM((2, A, block, cols), BF16),
            pltpu.VMEM((2, block, cols), F32),
            pltpu.VMEM((8, H * LANES), F32),
            pltpu.VMEM((8, cols), F32),
            pltpu.VMEM((2, 2, 8, LANES), F32),
            pltpu.VMEM((B, 2, 8, LANES), F32),
            pltpu.VMEM((A, 2, 8, LANES), F32),
            dma,
            dma((G,)),
            dma((2,)),
            dma((4, G, N)),
            dma((G, N, pieces)),
            dma((2, H)),
            dma((2, H)),
            dma((G, tiles, H)),
            dma((G, tiles, H)),
            dma((2, tiles)),
            dma((2, tiles)),
            dma((2, A, B)),
            dma((2, A, B)),
            dma((2, A)),
            dma((2, A)),
            dma((1 + A + B,)),
            dma,
            dma((B,)),
            dma((A,)),
        ],
        compiler_params=pltpu.CompilerParams(
            collective_id=0, has_side_effects=True, vmem_limit_bytes=54912 * 2**10
        ),
    )(
        freqs, positions.reshape(rows // LANES, LANES), hidden, weight,
        down.reshape(G, LANES, rank), up,
    )


def solution(mesh):
    N, H = mesh.shape["seq"], mesh.shape["head"]

    def per_device(hidden, key_value_weight, down_projection, up_projection, positions):
        grad_down, grad_up, rel = fused(
            N, H, frequencies(), positions, hidden, key_value_weight, down_projection, up_projection
        )
        return grad_down, grad_up, rel[0, 0]

    return jax.shard_map(
        per_device,
        mesh=mesh,
        in_specs=(P("seq", None), P("seq", "head"), P("head", None), P(None, "head"), P("seq")),
        out_specs=(P("seq", "head"), P("seq", "head"), P()),
        check_vma=False,
    )
```

```python
import functools
import math

import jax
import jax.numpy as jnp
from jax import lax
from jax.experimental import pallas as pl
from jax.experimental.pallas import tpu as pltpu
from jax.sharding import PartitionSpec as P

KEY_VALUE_HEADS = 8
HEAD_SIZE = 128
THETA = 500000.0
MESH = pl.DeviceIdType.MESH
BF16 = jnp.bfloat16
F32 = jnp.float32
LANES = 128


def frequencies():
    half_dim = HEAD_SIZE // 2
    freqs = jnp.power(
        jnp.float32(THETA), -(jnp.arange(half_dim, dtype=jnp.float32) * 2.0 / HEAD_SIZE)
    )
    return jnp.concatenate([freqs, freqs])[None, :]


def cut(depth, B, pieces):
    if B > 2 or depth < 512:
        return (0, depth), depth
    late = depth - depth * 13 // 64 // 16 * 16
    bounds = [-(-(late * i // pieces) // 16) * 16 for i in range(pieces)]
    return tuple(bounds) + (late, depth), late


def kernel(
    A, B, H, coarse, fine, late, entry_items, token_count,
    freq_ref, pos_ref, hidden_ref, weight_ref, down_ref, up_ref,
    gd_ref, gu_ref, rel_ref,
    hid, wbuf, acc, cosine, sine, own_t, all_t, downs, ups, lat_acc, lat, dlat, res, res_o,
    grad, gs1, gr1, gs2, gr2, fin, esum, msum, e0, e1, e2,
    hid_sem, own_sem, mat_sem, send_sem, recv_sem, m_send, m_recv, x_send, x_recv,
    l_send, l_recv, g1_send, g1_recv, g2_send, g2_recv, e_send, e0_recv, e1_recv, e2_recv,
):
    s, h = lax.axis_index("seq"), lax.axis_index("head")
    a, b = s // B, s % B
    y, core = h // 2, h % 2
    other = 1 - core
    sib = y * 2 + other
    N = A * B
    G, _, depth, _ = wbuf.shape
    rows = hid.shape[0]
    tiles, tile = own_t.shape[2:4]
    rank = downs.shape[3]
    cols = ups.shape[2]

    load = pltpu.make_async_copy(hidden_ref, hid, hid_sem)

    def own_load(g):
        return pltpu.make_async_copy(
            weight_ref.at[:, pl.ds(pl.multiple_of(g * LANES, LANES), LANES)],
            wbuf.at[g, s], own_sem.at[g],
        )

    own_load(0).start()
    own_load(1).start()
    mats = (
        pltpu.make_async_copy(down_ref, downs.at[:, h], mat_sem.at[0]),
        pltpu.make_async_copy(up_ref, ups.at[h], mat_sem.at[1]),
    )

    barrier = pltpu.get_barrier_semaphore()
    for j in range(1, H):
        pl.semaphore_signal(barrier, inc=1, device_id=(s, (h + j) % H), device_id_type=MESH)
    for j in range(1, A):
        pl.semaphore_signal(
            barrier, inc=1, device_id=((a + j) % A * B + b, h), device_id_type=MESH
        )
    for j in range(1, B):
        pl.semaphore_signal(
            barrier, inc=1, device_id=(a * B + (b + j) % B, h), device_id_type=MESH
        )
    load.start()
    for g in range(2, G):
        own_load(g).start()
    for m in mats:
        m.start()
    pl.semaphore_wait(barrier, H - 1 + A - 1 + B - 1)

    def remote(src, dst, ssem, rsem, peer):
        return pltpu.make_async_remote_copy(
            src_ref=src, dst_ref=dst, send_sem=ssem, recv_sem=rsem,
            device_id=peer, device_id_type=MESH,
        )

    ways = (
        (a + 1 < A, s + B),
        (a > 0, s - B),
        (b + 1 < B, s + 1),
        (b > 0, s - 1),
    )

    def part(way, peer, g, o, lo, hi, rsem):
        block = wbuf.at[g, o, pl.ds(lo, hi - lo)]
        return remote(block, block, send_sem.at[way, g, o], rsem, (peer, h))

    def forwards(da, db, g, o, i, bounds):
        first = bounds[i] >= late
        conds = (
            (da >= 0) & (first | (db == 0)),
            (da <= 0) & (first | (db == 0)),
            (db >= 0) & ((not first) | (da == 0)),
            (db <= 0) & ((not first) | (da == 0)),
        )
        for way in range(4):
            @pl.when(ways[way][0] & conds[way])
            def _():
                part(
                    way, ways[way][1], g, o, bounds[i], bounds[i + 1], recv_sem.at[g, o, i]
                ).start()

    def own_start(g, bounds):
        own_load(g).wait()
        for i in range(len(bounds) - 1):
            forwards(0, 0, g, s, i, bounds)

    def pieces_of(g):
        return fine if g == G - 1 else coarse

    own_start(0, pieces_of(0))
    own_start(1, pieces_of(1))

    def to_head(m, hh):
        if m == 0:
            return remote(down_ref, downs.at[:, h], m_send.at[0, hh], m_recv.at[0, h], (s, hh))
        return remote(up_ref, ups.at[h], m_send.at[1, hh], m_recv.at[1, h], (s, hh))

    def from_head(m, hh):
        if m == 0:
            return remote(down_ref, downs.at[:, hh], m_send.at[0, hh], m_recv.at[0, hh], (s, hh))
        return remote(up_ref, ups.at[hh], m_send.at[1, hh], m_recv.at[1, hh], (s, hh))

    for m in range(2):
        for j in range(1, H):
            to_head(m, (h + j) % H).start()

    lane = lax.broadcasted_iota(jnp.int32, (LANES, LANES), 1)
    low = lane < HEAD_SIZE // 2
    sign = jnp.where(low, -1.0, 1.0)
    pos = pos_ref[...].astype(F32)
    blocks = rows // LANES
    for i in range(blocks // 2):
        k = i + blocks // 2
        p1 = jnp.broadcast_to(pos[i : i + 1], (LANES, LANES)).T
        p2 = jnp.broadcast_to(pos[k : k + 1], (LANES, LANES)).T
        angle = jnp.where(low, p1, p2) * freq_ref[...]
        ca, sa = jnp.cos(angle), jnp.sin(angle)
        cr, sr = pltpu.roll(ca, HEAD_SIZE // 2, 1), pltpu.roll(sa, HEAD_SIZE // 2, 1)
        r1, r2 = slice(i * LANES, (i + 1) * LANES), slice(k * LANES, (k + 1) * LANES)
        cosine[r1] = jnp.where(low, ca, cr)
        cosine[r2] = jnp.where(low, cr, ca)
        sine[r1] = jnp.where(low, sa, sr) * sign
        sine[r2] = jnp.where(low, sr, sa) * sign
    esum[...] = jnp.zeros_like(esum)
    msum[...] = jnp.zeros_like(msum)
    lat_acc[...] = jnp.zeros_like(lat_acc)
    acc[...] = jnp.zeros_like(acc)
    load.wait()

    def product(g, o, lo, hi):
        start = pl.multiple_of(o * depth + lo, min(depth, 256))
        w = wbuf[g, o, lo:hi]
        step = 512
        for m in range(0, rows, step):
            acc[g, m : m + step] += jnp.dot(
                hid[m : m + step, pl.ds(start, hi - lo)], w, preferred_element_type=F32
            )

    def to_peer(g, r, hh):
        return remote(
            own_t.at[g, hh % 2, r], all_t.at[g, h, r], x_send.at[g, r, hh], x_recv.at[g, r, h],
            (s, hh),
        )

    def from_peer(g, r, hh):
        return remote(
            own_t.at[g, core, r], all_t.at[g, hh, r], x_send.at[g, r, hh], x_recv.at[g, r, hh],
            (s, hh),
        )

    def finish(g):
        is_key = (g % 2) == 0
        for c in range(2):
            for r in range(tiles):
                lo = (c * tiles + r) * tile

                @pl.when(is_key)
                def _():
                    key = acc[g, lo : lo + tile]
                    turned = key * cosine[lo : lo + tile] + pltpu.roll(
                        key, HEAD_SIZE // 2, 1
                    ) * sine[lo : lo + tile]
                    own_t[g, c, r] = turned.astype(BF16)

                @pl.when(jnp.logical_not(is_key))
                def _():
                    own_t[g, c, r] = acc[g, lo : lo + tile].astype(BF16)
        for r in range(tiles):
            all_t[g, h, r] = own_t[g, core, r]
        for r in range(tiles):
            for j in range(1, H):
                to_peer(g, r, (h + j) % H).start()

    def latent(g, r):
        for j in range(1, H):
            from_peer(g, r, (h + j) % H).wait_recv()
        x = jnp.concatenate([all_t[g, hh, r] for hh in range(H)], axis=1)
        d = downs[g].reshape(H * LANES, rank)
        lat_acc[r] += jnp.dot(x, d, preferred_element_type=F32)
        wide = x.astype(F32)
        esum[...] += jnp.sum((wide * wide).reshape(tile // 8, 8, H * LANES), axis=0)

    combos = 2 * (2 * B - 1)

    def combo(u, t):
        m = t // 2
        e = (m + 1) // 2
        off = (e if m % 2 == 1 else -e) if isinstance(m, int) else jnp.where(m % 2 == 1, e, -e)
        side = 1 - 2 * (t % 2)
        d = u + 1 - e
        a0, b0 = a + side * d, b + off
        ok = (d >= 0) & (a0 >= 0) & (a0 < A) & (b0 >= 0) & (b0 < B)
        ok = ok & ((d > 0) | (side > 0))
        return ok, a - a0, b - b0, a0 * B + b0

    last_stage = A + B - 3

    product(0, s, 0, depth)
    product(1, s, 0, depth)

    def arrivals(g, u, bounds):
        spans = [bound // 256 * 256 for bound in bounds[:-1]] + [depth]
        for i in range(len(bounds) - 1):
            for t in range(combos):
                ok, da, db, o = combo(u, t)

                @pl.when(ok)
                def _():
                    part(
                        0, s, g, o, bounds[i], bounds[i + 1], recv_sem.at[g, o, i]
                    ).wait_recv()
                    forwards(da, db, g, o, i, bounds)
            def multiply(t, carry):
                ok, _, _, o = combo(u, t)

                @pl.when(ok)
                def _():
                    product(g, o, spans[i], spans[i + 1])
                return carry
            lax.fori_loop(0, combos, multiply, 0)

    def step(tau, carry):
        def group(g, carry):
            u = tau - g

            @pl.when((u >= 0) & (u <= last_stage))
            def _():
                arrivals(g, u, coarse)

            @pl.when(u == last_stage)
            def _():
                finish(g)

            @pl.when((u == last_stage) & (g == 0))
            def _():
                mats[0].wait()
                for j in range(1, H):
                    from_head(0, (h + j) % H).wait_recv()

            @pl.when((u == last_stage) & (g > 0))
            def _():
                for r in range(tiles):
                    latent(jnp.maximum(g - 1, 0), r)

            @pl.when((u == -2) & (g > 1))
            def _():
                own_start(g, coarse)
                product(g, s, 0, depth)
            return carry
        lax.fori_loop(0, G - 1, group, 0)
        u = tau - last

        @pl.when((u >= 0) & (u <= last_stage))
        def _():
            arrivals(last, u, fine)

        if last > 1:
            @pl.when(u == -2)
            def _():
                own_start(last, fine)
                product(last, s, 0, depth)
        return carry
    last = G - 1
    lax.fori_loop(0, last_stage + G, step, 0)

    def nt(x, w):
        return lax.dot_general(x, w, (((1,), (1,)), ((), ())), preferred_element_type=F32)

    def tn(x, w):
        return lax.dot_general(x, w, (((0,), (0,)), ((), ())), preferred_element_type=F32)

    def to_sib(k, r, c):
        buf = (lat, dlat)[k].at[c, r]
        return remote(buf, buf, l_send.at[k, r], l_recv.at[k, r], (s, sib))

    finish(last)
    for r in range(tiles):
        latent(last - 1, r)
    mats[1].wait()
    for j in range(1, H):
        from_head(1, (h + j) % H).wait_recv()

    def columns(ref, *at):
        return jnp.concatenate([ref[(g,) + at] for g in range(G)], axis=1)

    def misfit(hh, r):
        left = columns(all_t, hh, r).astype(F32) - jnp.dot(
            lat[core, r], ups[hh], preferred_element_type=F32
        )
        res[hh, r] = left.astype(BF16)
        msum[hh] += jnp.sum((left * left).reshape(tile // 8, 8, cols), axis=0)

    def rest(r):
        for j in range(1, H):
            misfit((h + j) % H, r)
        total = nt(res[0, r], ups[0])
        for hh in range(1, H):
            total += nt(res[hh, r], ups[hh])
        dlat[core, r] = total.astype(BF16)
        to_sib(1, r, core).start()

    for r in range(tiles):
        latent(last, r)
        lat[core, r] = lat_acc[r].astype(BF16)
        to_sib(0, r, core).start()
        misfit(h, r)

    small = e0.shape[-2:]
    def level0(c):
        return remote(e0.at[c], e0.at[c], e_send.at[0], e0_recv, (s, sib))

    def level1(bb, slot):
        return remote(e1.at[slot], e1.at[slot], e_send.at[1 + bb], e1_recv.at[slot], (a * B + bb, h))

    def level2(aa, slot):
        return remote(
            e2.at[slot], e2.at[slot], e_send.at[1 + B + aa], e2_recv.at[slot], (aa * B + b, h)
        )

    def first_hop(k, aa, bb, slot):
        return remote(
            gs1.at[k, aa, bb], gr1.at[k, aa, slot], g1_send.at[k, aa, bb], g1_recv.at[k, aa, slot],
            (a * B + bb, h),
        )

    def second_hop(k, aa, slot):
        return remote(
            gs2.at[k, aa], gr2.at[k, slot], g2_send.at[k, aa], g2_recv.at[k, slot],
            (aa * B + b, h),
        )

    def scatter(k, value):
        value = value.reshape(grad.shape[1:])
        grad[k] = value
        gs1[k] = value.astype(BF16)
        for i in range(1, A + 1):
            for j in range(1, B):
                first_hop(k, (a + i) % A, (b + j) % B, b).start()

    def combine(k):
        for i in range(1, A + 1):
            aa = (a + i) % A
            total = grad[k, aa, b]
            for j in range(1, B):
                bb = (b + j) % B
                first_hop(k, aa, bb, bb).wait_recv()
                total += gr1[k, aa, bb].astype(F32)
            if i < A:
                gs2[k, aa] = total.astype(BF16)
                second_hop(k, aa, a).start()
            else:
                fin[k] = total

    for r in range(tiles):
        to_sib(0, r, other).wait_recv()
        left = columns(own_t, other, r).astype(F32) - jnp.dot(
            lat[other, r], ups[h], preferred_element_type=F32
        )
        res_o[r] = left.astype(BF16)
    half = tiles * tile
    scatter(
        0,
        tn(lat[core].reshape(half, rank), res[h].reshape(half, cols))
        + tn(lat[other].reshape(half, rank), res_o[...].reshape(half, cols)),
    )

    for r in range(tiles):
        rest(r)
    total = msum[0]
    for hh in range(1, H):
        total += msum[hh]
    e0[core, 0] = jnp.full(small, jnp.sum(esum[...]), F32)
    e0[core, 1] = jnp.full(small, jnp.sum(total), F32)
    level0(core).start()

    def targets(c):
        return jnp.concatenate(
            [own_t[g, c].reshape(half, LANES) for g in range(G)], axis=1
        )

    mine = tn(dlat[core].reshape(half, rank), targets(core))
    for r in range(tiles):
        to_sib(1, r, other).wait_recv()
    scatter(1, mine + tn(dlat[other].reshape(half, rank), targets(other)))

    level0(other).wait_recv()
    e1[b] = e0[0] + e0[1]
    for j in range(1, B):
        level1((b + j) % B, b).start()

    combine(0)

    for j in range(1, B):
        bb = (b + j) % B
        level1(bb, bb).wait_recv()
    total = e1[0]
    for bb in range(1, B):
        total += e1[bb]
    e2[a] = total
    for j in range(1, A):
        level2((a + j) % A, a).start()

    combine(1)

    def sends(n, carry):
        g, o = n // N, n % N
        da, db = a - o // B, b - o % B
        zs = (da >= 0, da <= 0)
        xs = (db >= 0, db <= 0)
        for way in range(2):
            @pl.when(ways[way][0] & zs[way] & (db == 0))
            def _():
                part(way, s, g, o, 0, depth, recv_sem.at[g, o, 0]).wait_send()
            if late < depth:
                @pl.when(ways[way][0] & zs[way] & (db != 0))
                def _():
                    part(way, s, g, o, late, depth, recv_sem.at[g, o, 0]).wait_send()
        for way in range(2, 4):
            @pl.when(ways[way][0] & xs[way - 2] & (da == 0))
            def _():
                part(way, s, g, o, 0, depth, recv_sem.at[g, o, 0]).wait_send()

            @pl.when(ways[way][0] & xs[way - 2] & (da != 0))
            def _():
                part(way, s, g, o, 0, late, recv_sem.at[g, o, 0]).wait_send()
        return carry
    lax.fori_loop(0, G * N, sends, 0)
    for j in range(1, H):
        hh = (h + j) % H
        for m in range(2):
            to_head(m, hh).wait_send()
        for r in range(tiles):
            for g in range(G):
                to_peer(g, r, hh).wait_send()
    for k in range(2):
        for r in range(tiles):
            to_sib(k, r, core).wait_send()
        for i in range(1, A + 1):
            for j in range(1, B):
                first_hop(k, (a + i) % A, (b + j) % B, b).wait_send()
    level0(core).wait_send()
    for j in range(1, B):
        level1((b + j) % B, b).wait_send()

    for j in range(1, A):
        aa = (a + j) % A
        level2(aa, aa).wait_recv()
    total = e2[0]
    for aa in range(1, A):
        total += e2[aa]
    whole_energy, whole_misfit = total[0], total[1]
    rel_ref[...] = whole_misfit / whole_energy
    factor = (-(entry_items / whole_energy) / math.sqrt(token_count))[0:1, 0:1]

    for k, out in ((0, gu_ref), (1, gd_ref)):
        total = fin[k]
        for i in range(1, A):
            aa = (a + i) % A
            second_hop(k, aa, aa).wait_recv()
            total += gr2[k, aa].astype(F32)
        out[...] = factor * total
    for k in range(2):
        for i in range(1, A):
            second_hop(k, (a + i) % A, a).wait_send()
    for j in range(1, A):
        level2((a + j) % A, a).wait_send()


def fused(N, H, freqs, positions, hidden, weight, down, up):
    B = 2 if N <= 8 else 8
    A = N // B
    rows, width = hidden.shape
    depth, cols = weight.shape
    rank = down.shape[1]
    G = cols // LANES
    block = rank // N
    tiles = 2
    tile = rows // 2 // tiles
    coarse, late = cut(depth, B, 1)
    fine, _ = cut(depth, B, 2)
    pieces = len(fine) - 1
    token_count = N * rows
    dma = pltpu.SemaphoreType.DMA
    vmem = pl.BlockSpec(memory_space=pltpu.VMEM)
    hbm = pl.BlockSpec(memory_space=pltpu.HBM)
    return pl.pallas_call(
        functools.partial(
            kernel, A, B, H, coarse, fine, late,
            token_count * 2 * KEY_VALUE_HEADS * HEAD_SIZE, token_count,
        ),
        out_shape=(
            jax.ShapeDtypeStruct((block, cols), F32),
            jax.ShapeDtypeStruct((block, cols), F32),
            jax.ShapeDtypeStruct((8, LANES), F32),
        ),
        in_specs=[vmem] * 2 + [hbm] * 4,
        out_specs=(vmem,) * 3,
        scratch_shapes=[
            pltpu.VMEM((rows, width), BF16),
            pltpu.VMEM((G, N, depth, LANES), BF16),
            pltpu.VMEM((G, rows, LANES), F32),
            pltpu.VMEM((rows, LANES), F32),
            pltpu.VMEM((rows, LANES), F32),
            pltpu.VMEM((G, 2, tiles, tile, LANES), BF16),
            pltpu.VMEM((G, H, tiles, tile, LANES), BF16),
            pltpu.VMEM((G, H, LANES, rank), BF16),
            pltpu.VMEM((H, rank, cols), BF16),
            pltpu.VMEM((tiles, tile, rank), F32),
            pltpu.VMEM((2, tiles, tile, rank), BF16),
            pltpu.VMEM((2, tiles, tile, rank), BF16),
            pltpu.VMEM((H, tiles, tile, cols), BF16),
            pltpu.VMEM((tiles, tile, cols), BF16),
            pltpu.VMEM((2, A, B, block, cols), F32),
            pltpu.VMEM((2, A, B, block, cols), BF16),
            pltpu.VMEM((2, A, B, block, cols), BF16),
            pltpu.VMEM((2, A, block, cols), BF16),
            pltpu.VMEM((2, A, block, cols), BF16),
            pltpu.VMEM((2, block, cols), F32),
            pltpu.VMEM((8, H * LANES), F32),
            pltpu.VMEM((H, 8, cols), F32),
            pltpu.VMEM((2, 2, 8, LANES), F32),
            pltpu.VMEM((B, 2, 8, LANES), F32),
            pltpu.VMEM((A, 2, 8, LANES), F32),
            dma,
            dma((G,)),
            dma((2,)),
            dma((4, G, N)),
            dma((G, N, pieces)),
            dma((2, H)),
            dma((2, H)),
            dma((G, tiles, H)),
            dma((G, tiles, H)),
            dma((2, tiles)),
            dma((2, tiles)),
            dma((2, A, B)),
            dma((2, A, B)),
            dma((2, A)),
            dma((2, A)),
            dma((1 + A + B,)),
            dma,
            dma((B,)),
            dma((A,)),
        ],
        compiler_params=pltpu.CompilerParams(
            collective_id=0, has_side_effects=True, vmem_limit_bytes=54912 * 2**10
        ),
    )(
        freqs, positions.reshape(rows // LANES, LANES), hidden, weight,
        down.reshape(G, LANES, rank), up,
    )


def solution(mesh):
    N, H = mesh.shape["seq"], mesh.shape["head"]

    def per_device(hidden, key_value_weight, down_projection, up_projection, positions):
        grad_down, grad_up, rel = fused(
            N, H, frequencies(), positions, hidden, key_value_weight, down_projection, up_projection
        )
        return grad_down, grad_up, rel[0, 0]

    return jax.shard_map(
        per_device,
        mesh=mesh,
        in_specs=(P("seq", None), P("seq", "head"), P("head", None), P(None, "head"), P("seq")),
        out_specs=(P("seq", "head"), P("seq", "head"), P()),
        check_vma=False,
    )
```

```python
import functools
import math

import jax
import jax.numpy as jnp
from jax import lax
from jax.experimental import pallas as pl
from jax.experimental.pallas import tpu as pltpu
from jax.sharding import PartitionSpec as P

KEY_VALUE_HEADS = 8
HEAD_SIZE = 128
THETA = 500000.0
MESH = pl.DeviceIdType.MESH
BF16 = jnp.bfloat16
F32 = jnp.float32
LANES = 128
PIECES = 2


def frequencies():
    half_dim = HEAD_SIZE // 2
    freqs = jnp.power(
        jnp.float32(THETA), -(jnp.arange(half_dim, dtype=jnp.float32) * 2.0 / HEAD_SIZE)
    )
    return jnp.concatenate([freqs, freqs])[None, :]


def cut(depth, B):
    count = PIECES
    if B > 2 or depth < 512:
        return (0, depth), depth
    late = depth - depth * 13 // 64 // 16 * 16
    bounds = [-(-(late * i // (count - 1)) // 16) * 16 for i in range(count - 1)]
    return tuple(bounds) + (late, depth), late


def kernel(
    A, B, H, bounds, late, entry_items, token_count,
    freq_ref, pos_ref, hidden_ref, weight_ref, down_ref, up_ref,
    gd_ref, gu_ref, rel_ref,
    hid, wbuf, acc, cosine, sine, own_t, all_t, downs, ups, lat_acc, lat, dlat, res, res_o,
    grad, gs1, gr1, gs2, gr2, fin, esum, msum, e0, e1, e2,
    hid_sem, own_sem, mat_sem, send_sem, recv_sem, m_send, m_recv, x_send, x_recv,
    l_send, l_recv, g1_send, g1_recv, g2_send, g2_recv, e_send, e0_recv, e1_recv, e2_recv,
):
    s, h = lax.axis_index("seq"), lax.axis_index("head")
    a, b = s // B, s % B
    y, core = h // 2, h % 2
    other = 1 - core
    sib = y * 2 + other
    N = A * B
    G, _, depth, _ = wbuf.shape
    rows = hid.shape[0]
    tiles, tile = own_t.shape[2:4]
    rank = downs.shape[3]
    cols = ups.shape[2]
    pieces = len(bounds) - 1
    spans = [bound // 256 * 256 for bound in bounds[:-1]] + [depth]

    load = pltpu.make_async_copy(hidden_ref, hid, hid_sem)

    def own_load(g):
        return pltpu.make_async_copy(
            weight_ref.at[:, pl.ds(pl.multiple_of(g * LANES, LANES), LANES)],
            wbuf.at[g, s], own_sem.at[g],
        )

    own_load(0).start()
    own_load(1).start()
    mats = (
        pltpu.make_async_copy(down_ref, downs.at[:, h], mat_sem.at[0]),
        pltpu.make_async_copy(up_ref, ups.at[h], mat_sem.at[1]),
    )

    barrier = pltpu.get_barrier_semaphore()
    for j in range(1, H):
        pl.semaphore_signal(barrier, inc=1, device_id=(s, (h + j) % H), device_id_type=MESH)
    for j in range(1, A):
        pl.semaphore_signal(
            barrier, inc=1, device_id=((a + j) % A * B + b, h), device_id_type=MESH
        )
    for j in range(1, B):
        pl.semaphore_signal(
            barrier, inc=1, device_id=(a * B + (b + j) % B, h), device_id_type=MESH
        )
    load.start()
    for g in range(2, G):
        own_load(g).start()
    for m in mats:
        m.start()
    pl.semaphore_wait(barrier, H - 1 + A - 1 + B - 1)

    def remote(src, dst, ssem, rsem, peer):
        return pltpu.make_async_remote_copy(
            src_ref=src, dst_ref=dst, send_sem=ssem, recv_sem=rsem,
            device_id=peer, device_id_type=MESH,
        )

    ways = (
        (a + 1 < A, s + B),
        (a > 0, s - B),
        (b + 1 < B, s + 1),
        (b > 0, s - 1),
    )

    def part(way, peer, g, o, lo, hi, rsem):
        block = wbuf.at[g, o, pl.ds(lo, hi - lo)]
        return remote(block, block, send_sem.at[way, g, o], rsem, (peer, h))

    def forwards(da, db, g, o, i):
        first = bounds[i] >= late
        conds = (
            (da >= 0) & (first | (db == 0)),
            (da <= 0) & (first | (db == 0)),
            (db >= 0) & ((not first) | (da == 0)),
            (db <= 0) & ((not first) | (da == 0)),
        )
        for way in range(4):
            @pl.when(ways[way][0] & conds[way])
            def _():
                part(
                    way, ways[way][1], g, o, bounds[i], bounds[i + 1], recv_sem.at[g, o, i]
                ).start()

    def own_start(g):
        own_load(g).wait()
        for i in range(pieces):
            forwards(0, 0, g, s, i)

    own_start(0)
    own_start(1)

    def to_head(m, hh):
        if m == 0:
            return remote(down_ref, downs.at[:, h], m_send.at[0, hh], m_recv.at[0, h], (s, hh))
        return remote(up_ref, ups.at[h], m_send.at[1, hh], m_recv.at[1, h], (s, hh))

    def from_head(m, hh):
        if m == 0:
            return remote(down_ref, downs.at[:, hh], m_send.at[0, hh], m_recv.at[0, hh], (s, hh))
        return remote(up_ref, ups.at[hh], m_send.at[1, hh], m_recv.at[1, hh], (s, hh))

    for m in range(2):
        for j in range(1, H):
            to_head(m, (h + j) % H).start()

    lane = lax.broadcasted_iota(jnp.int32, (LANES, LANES), 1)
    low = lane < HEAD_SIZE // 2
    sign = jnp.where(low, -1.0, 1.0)
    pos = pos_ref[...].astype(F32)
    blocks = rows // LANES
    for i in range(blocks // 2):
        k = i + blocks // 2
        p1 = jnp.broadcast_to(pos[i : i + 1], (LANES, LANES)).T
        p2 = jnp.broadcast_to(pos[k : k + 1], (LANES, LANES)).T
        angle = jnp.where(low, p1, p2) * freq_ref[...]
        ca, sa = jnp.cos(angle), jnp.sin(angle)
        cr, sr = pltpu.roll(ca, HEAD_SIZE // 2, 1), pltpu.roll(sa, HEAD_SIZE // 2, 1)
        r1, r2 = slice(i * LANES, (i + 1) * LANES), slice(k * LANES, (k + 1) * LANES)
        cosine[r1] = jnp.where(low, ca, cr)
        cosine[r2] = jnp.where(low, cr, ca)
        sine[r1] = jnp.where(low, sa, sr) * sign
        sine[r2] = jnp.where(low, sr, sa) * sign
    esum[...] = jnp.zeros_like(esum)
    msum[...] = jnp.zeros_like(msum)
    lat_acc[...] = jnp.zeros_like(lat_acc)
    acc[...] = jnp.zeros_like(acc)
    load.wait()

    def product(g, o, q):
        lo, span = spans[q], spans[q + 1] - spans[q]
        start = pl.multiple_of(o * depth + lo, min(span, 256))
        w = wbuf[g, o, lo : lo + span]
        step = 512
        for m in range(0, rows, step):
            acc[g, m : m + step] += jnp.dot(
                hid[m : m + step, pl.ds(start, span)], w, preferred_element_type=F32
            )

    def to_peer(g, r, hh):
        return remote(
            own_t.at[g, hh % 2, r], all_t.at[g, h, r], x_send.at[g, r, hh], x_recv.at[g, r, h],
            (s, hh),
        )

    def from_peer(g, r, hh):
        return remote(
            own_t.at[g, core, r], all_t.at[g, hh, r], x_send.at[g, r, hh], x_recv.at[g, r, hh],
            (s, hh),
        )

    def finish(g):
        is_key = (g % 2) == 0
        for c in range(2):
            for r in range(tiles):
                lo = (c * tiles + r) * tile

                @pl.when(is_key)
                def _():
                    key = acc[g, lo : lo + tile]
                    turned = key * cosine[lo : lo + tile] + pltpu.roll(
                        key, HEAD_SIZE // 2, 1
                    ) * sine[lo : lo + tile]
                    own_t[g, c, r] = turned.astype(BF16)

                @pl.when(jnp.logical_not(is_key))
                def _():
                    own_t[g, c, r] = acc[g, lo : lo + tile].astype(BF16)
        for r in range(tiles):
            all_t[g, h, r] = own_t[g, core, r]
        for r in range(tiles):
            for j in range(1, H):
                to_peer(g, r, (h + j) % H).start()

    def latent(g, r):
        for j in range(1, H):
            from_peer(g, r, (h + j) % H).wait_recv()
        x = jnp.concatenate([all_t[g, hh, r] for hh in range(H)], axis=1)
        d = downs[g].reshape(H * LANES, rank)
        lat_acc[r] += jnp.dot(x, d, preferred_element_type=F32)
        wide = x.astype(F32)
        esum[...] += jnp.sum((wide * wide).reshape(tile // 8, 8, H * LANES), axis=0)

    combos = 2 * (2 * B - 1)

    def combo(u, t):
        m = t // 2
        e = (m + 1) // 2
        off = e if m % 2 == 1 else -e
        side = 1 - 2 * (t % 2)
        d = u + 1 - e
        a0, b0 = a + side * d, b + off
        ok = (d >= 0) & (a0 >= 0) & (a0 < A) & (b0 >= 0) & (b0 < B)
        ok = ok & ((d > 0) | (side > 0))
        return ok, a - a0, b - b0, a0 * B + b0

    last_stage = A + B - 3

    def begin(g):
        for q in range(pieces):
            product(g, s, q)

    begin(0)
    begin(1)

    def arrivals(g, u):
        for i in range(pieces):
            def arrive(t, carry):
                ok, da, db, o = combo(u, t)

                @pl.when(ok)
                def _():
                    part(
                        0, s, g, o, bounds[i], bounds[i + 1], recv_sem.at[g, o, i]
                    ).wait_recv()
                    forwards(da, db, g, o, i)
                return carry
            [arrive(t, 0) for t in range(combos)]

            def multiply(t, carry):
                ok, _, _, o = combo(u, t)

                @pl.when(ok)
                def _():
                    product(g, o, i)
                return carry
            [multiply(t, 0) for t in range(combos)]

    def step(tau, carry):
        def group(g, carry):
            u = tau - g

            @pl.when((u >= 0) & (u <= last_stage))
            def _():
                arrivals(g, u)

            @pl.when((u == last_stage) & (g < G - 1))
            def _():
                finish(g)

            @pl.when((u == last_stage) & (g == 0))
            def _():
                mats[0].wait()
                for j in range(1, H):
                    from_head(0, (h + j) % H).wait_recv()

            @pl.when((u == last_stage) & (g > 0) & (g < G - 1))
            def _():
                for r in range(tiles):
                    latent(jnp.maximum(g - 1, 0), r)

            @pl.when(u == -2)
            def _():
                own_start(g)
                begin(g)
            return carry
        return lax.fori_loop(0, G, group, carry)
    lax.fori_loop(0, last_stage + G, step, 0)

    def nt(x, w):
        return lax.dot_general(x, w, (((1,), (1,)), ((), ())), preferred_element_type=F32)

    def tn(x, w):
        return lax.dot_general(x, w, (((0,), (0,)), ((), ())), preferred_element_type=F32)

    def to_sib(k, r, c):
        buf = (lat, dlat)[k].at[c, r]
        return remote(buf, buf, l_send.at[k, r], l_recv.at[k, r], (s, sib))

    last = G - 1
    finish(last)
    for r in range(tiles):
        latent(last - 1, r)
    mats[1].wait()
    for j in range(1, H):
        from_head(1, (h + j) % H).wait_recv()

    def columns(ref, *at):
        return jnp.concatenate([ref[(g,) + at] for g in range(G)], axis=1)

    for r in range(tiles):
        latent(last, r)
        narrow = lat_acc[r].astype(BF16)
        lat[core, r] = narrow
        to_sib(0, r, core).start()
        for hh in range(H):
            left = columns(all_t, hh, r).astype(F32) - jnp.dot(
                narrow, ups[hh], preferred_element_type=F32
            )
            res[hh, r] = left.astype(BF16)
            msum[...] += jnp.sum((left * left).reshape(tile // 8, 8, cols), axis=0)

    small = e0.shape[-2:]
    e0[core, 0] = jnp.full(small, jnp.sum(esum[...]), F32)
    e0[core, 1] = jnp.full(small, jnp.sum(msum[...]), F32)

    def level0(c):
        return remote(e0.at[c], e0.at[c], e_send.at[0], e0_recv, (s, sib))

    def level1(bb, slot):
        return remote(e1.at[slot], e1.at[slot], e_send.at[1 + bb], e1_recv.at[slot], (a * B + bb, h))

    def level2(aa, slot):
        return remote(
            e2.at[slot], e2.at[slot], e_send.at[1 + B + aa], e2_recv.at[slot], (aa * B + b, h)
        )

    level0(core).start()

    def first_hop(k, aa, bb, slot):
        return remote(
            gs1.at[k, aa, bb], gr1.at[k, aa, slot], g1_send.at[k, aa, bb], g1_recv.at[k, aa, slot],
            (a * B + bb, h),
        )

    def second_hop(k, aa, slot):
        return remote(
            gs2.at[k, aa], gr2.at[k, slot], g2_send.at[k, aa], g2_recv.at[k, slot],
            (aa * B + b, h),
        )

    def scatter(k, value):
        value = value.reshape(grad.shape[1:])
        grad[k] = value
        gs1[k] = value.astype(BF16)
        for i in range(1, A + 1):
            for j in range(1, B):
                first_hop(k, (a + i) % A, (b + j) % B, b).start()

    def combine(k):
        for i in range(1, A + 1):
            aa = (a + i) % A
            total = grad[k, aa, b]
            for j in range(1, B):
                bb = (b + j) % B
                first_hop(k, aa, bb, bb).wait_recv()
                total += gr1[k, aa, bb].astype(F32)
            if i < A:
                gs2[k, aa] = total.astype(BF16)
                second_hop(k, aa, a).start()
            else:
                fin[k] = total

    for r in range(tiles):
        to_sib(0, r, other).wait_recv()
        left = columns(own_t, other, r).astype(F32) - jnp.dot(
            lat[other, r], ups[h], preferred_element_type=F32
        )
        res_o[r] = left.astype(BF16)
    half = tiles * tile
    scatter(
        0,
        tn(lat[core].reshape(half, rank), res[h].reshape(half, cols))
        + tn(lat[other].reshape(half, rank), res_o[...].reshape(half, cols)),
    )

    for r in range(tiles):
        total = nt(res[0, r], ups[0])
        for hh in range(1, H):
            total += nt(res[hh, r], ups[hh])
        dlat[core, r] = total.astype(BF16)
        to_sib(1, r, core).start()

    level0(other).wait_recv()
    e1[b] = e0[0] + e0[1]
    for j in range(1, B):
        level1((b + j) % B, b).start()

    def targets(c):
        return jnp.concatenate(
            [own_t[g, c].reshape(half, LANES) for g in range(G)], axis=1
        )

    mine = tn(dlat[core].reshape(half, rank), targets(core))
    for r in range(tiles):
        to_sib(1, r, other).wait_recv()
    scatter(1, mine + tn(dlat[other].reshape(half, rank), targets(other)))

    total = None
    for j in range(1, B):
        bb = (b + j) % B
        level1(bb, bb).wait_recv()
    total = e1[0]
    for bb in range(1, B):
        total += e1[bb]
    e2[a] = total
    for j in range(1, A):
        level2((a + j) % A, a).start()

    combine(0)
    combine(1)

    def sends(n, carry):
        g, o = n // N, n % N
        da, db = a - o // B, b - o % B
        zs = (da >= 0, da <= 0)
        xs = (db >= 0, db <= 0)
        for way in range(2):
            @pl.when(ways[way][0] & zs[way] & (db == 0))
            def _():
                part(way, s, g, o, 0, depth, recv_sem.at[g, o, 0]).wait_send()
            if late < depth:
                @pl.when(ways[way][0] & zs[way] & (db != 0))
                def _():
                    part(way, s, g, o, late, depth, recv_sem.at[g, o, 0]).wait_send()
        for way in range(2, 4):
            @pl.when(ways[way][0] & xs[way - 2] & (da == 0))
            def _():
                part(way, s, g, o, 0, depth, recv_sem.at[g, o, 0]).wait_send()

            @pl.when(ways[way][0] & xs[way - 2] & (da != 0))
            def _():
                part(way, s, g, o, 0, late, recv_sem.at[g, o, 0]).wait_send()
        return carry
    lax.fori_loop(0, G * N, sends, 0)
    for j in range(1, H):
        hh = (h + j) % H
        for m in range(2):
            to_head(m, hh).wait_send()
        for r in range(tiles):
            for g in range(G):
                to_peer(g, r, hh).wait_send()
    for k in range(2):
        for r in range(tiles):
            to_sib(k, r, core).wait_send()
        for i in range(1, A + 1):
            for j in range(1, B):
                first_hop(k, (a + i) % A, (b + j) % B, b).wait_send()
    level0(core).wait_send()
    for j in range(1, B):
        level1((b + j) % B, b).wait_send()

    for j in range(1, A):
        aa = (a + j) % A
        level2(aa, aa).wait_recv()
    total = e2[0]
    for aa in range(1, A):
        total += e2[aa]
    whole_energy, whole_misfit = total[0], total[1]
    rel_ref[...] = whole_misfit / whole_energy
    factor = (-(entry_items / whole_energy) / math.sqrt(token_count))[0:1, 0:1]

    for k, out in ((0, gu_ref), (1, gd_ref)):
        total = fin[k]
        for i in range(1, A):
            aa = (a + i) % A
            second_hop(k, aa, aa).wait_recv()
            total += gr2[k, aa].astype(F32)
        out[...] = factor * total
    for k in range(2):
        for i in range(1, A):
            second_hop(k, (a + i) % A, a).wait_send()
    for j in range(1, A):
        level2((a + j) % A, a).wait_send()


def fused(N, H, freqs, positions, hidden, weight, down, up):
    B = 2 if N <= 8 else 8
    A = N // B
    rows, width = hidden.shape
    depth, cols = weight.shape
    rank = down.shape[1]
    G = cols // LANES
    block = rank // N
    tiles = 2
    tile = rows // 2 // tiles
    bounds, late = cut(depth, B)
    pieces = len(bounds) - 1
    token_count = N * rows
    dma = pltpu.SemaphoreType.DMA
    vmem = pl.BlockSpec(memory_space=pltpu.VMEM)
    hbm = pl.BlockSpec(memory_space=pltpu.HBM)
    return pl.pallas_call(
        functools.partial(
            kernel, A, B, H, bounds, late,
            token_count * 2 * KEY_VALUE_HEADS * HEAD_SIZE, token_count,
        ),
        out_shape=(
            jax.ShapeDtypeStruct((block, cols), F32),
            jax.ShapeDtypeStruct((block, cols), F32),
            jax.ShapeDtypeStruct((8, LANES), F32),
        ),
        in_specs=[vmem] * 2 + [hbm] * 4,
        out_specs=(vmem,) * 3,
        scratch_shapes=[
            pltpu.VMEM((rows, width), BF16),
            pltpu.VMEM((G, N, depth, LANES), BF16),
            pltpu.VMEM((G, rows, LANES), F32),
            pltpu.VMEM((rows, LANES), F32),
            pltpu.VMEM((rows, LANES), F32),
            pltpu.VMEM((G, 2, tiles, tile, LANES), BF16),
            pltpu.VMEM((G, H, tiles, tile, LANES), BF16),
            pltpu.VMEM((G, H, LANES, rank), BF16),
            pltpu.VMEM((H, rank, cols), BF16),
            pltpu.VMEM((tiles, tile, rank), F32),
            pltpu.VMEM((2, tiles, tile, rank), BF16),
            pltpu.VMEM((2, tiles, tile, rank), BF16),
            pltpu.VMEM((H, tiles, tile, cols), BF16),
            pltpu.VMEM((tiles, tile, cols), BF16),
            pltpu.VMEM((2, A, B, block, cols), F32),
            pltpu.VMEM((2, A, B, block, cols), BF16),
            pltpu.VMEM((2, A, B, block, cols), BF16),
            pltpu.VMEM((2, A, block, cols), BF16),
            pltpu.VMEM((2, A, block, cols), BF16),
            pltpu.VMEM((2, block, cols), F32),
            pltpu.VMEM((8, H * LANES), F32),
            pltpu.VMEM((8, cols), F32),
            pltpu.VMEM((2, 2, 8, LANES), F32),
            pltpu.VMEM((B, 2, 8, LANES), F32),
            pltpu.VMEM((A, 2, 8, LANES), F32),
            dma,
            dma((G,)),
            dma((2,)),
            dma((4, G, N)),
            dma((G, N, pieces)),
            dma((2, H)),
            dma((2, H)),
            dma((G, tiles, H)),
            dma((G, tiles, H)),
            dma((2, tiles)),
            dma((2, tiles)),
            dma((2, A, B)),
            dma((2, A, B)),
            dma((2, A)),
            dma((2, A)),
            dma((1 + A + B,)),
            dma,
            dma((B,)),
            dma((A,)),
        ],
        compiler_params=pltpu.CompilerParams(
            collective_id=0, has_side_effects=True, vmem_limit_bytes=54912 * 2**10
        ),
    )(
        freqs, positions.reshape(rows // LANES, LANES), hidden, weight,
        down.reshape(G, LANES, rank), up,
    )


def solution(mesh):
    N, H = mesh.shape["seq"], mesh.shape["head"]

    def per_device(hidden, key_value_weight, down_projection, up_projection, positions):
        grad_down, grad_up, rel = fused(
            N, H, frequencies(), positions, hidden, key_value_weight, down_projection, up_projection
        )
        return grad_down, grad_up, rel[0, 0]

    return jax.shard_map(
        per_device,
        mesh=mesh,
        in_specs=(P("seq", None), P("seq", "head"), P("head", None), P(None, "head"), P("seq")),
        out_specs=(P("seq", "head"), P("seq", "head"), P()),
        check_vma=False,
    )
```

```python
import functools
import math

import jax
import jax.numpy as jnp
from jax import lax
from jax.experimental import pallas as pl
from jax.experimental.pallas import tpu as pltpu
from jax.sharding import PartitionSpec as P

KEY_VALUE_HEADS = 8
HEAD_SIZE = 128
THETA = 500000.0
MESH = pl.DeviceIdType.MESH
BF16 = jnp.bfloat16
F32 = jnp.float32
LANES = 128
PIECES = 2


def frequencies():
    half_dim = HEAD_SIZE // 2
    freqs = jnp.power(
        jnp.float32(THETA), -(jnp.arange(half_dim, dtype=jnp.float32) * 2.0 / HEAD_SIZE)
    )
    return jnp.concatenate([freqs, freqs])[None, :]


def cut(depth, B):
    count = PIECES
    if B > 2 or depth < 512:
        return (0, depth), depth
    late = depth - depth * 13 // 64 // 16 * 16
    bounds = [-(-(late * i // (count - 1)) // 16) * 16 for i in range(count - 1)]
    return tuple(bounds) + (late, depth), late


def kernel(
    A, B, H, bounds, late, entry_items, token_count,
    freq_ref, pos_ref, hidden_ref, weight_ref, down_ref, up_ref,
    gd_ref, gu_ref, rel_ref,
    hid, wbuf, acc, cosine, sine, own_t, all_t, downs, ups, lat_acc, lat, dlat, res, res_o,
    grad, gs1, gr1, gs2, gr2, fin, esum, msum, e0, e1, e2,
    hid_sem, own_sem, mat_sem, send_sem, recv_sem, m_send, m_recv, x_send, x_recv,
    l_send, l_recv, g1_send, g1_recv, g2_send, g2_recv, e_send, e0_recv, e1_recv, e2_recv,
):
    s, h = lax.axis_index("seq"), lax.axis_index("head")
    a, b = s // B, s % B
    y, core = h // 2, h % 2
    other = 1 - core
    sib = y * 2 + other
    N = A * B
    G, _, depth, _ = wbuf.shape
    rows = hid.shape[0]
    tiles, tile = own_t.shape[2:4]
    rank = downs.shape[3]
    cols = ups.shape[2]
    pieces = len(bounds) - 1
    spans = [bound // 256 * 256 for bound in bounds[:-1]] + [depth]

    load = pltpu.make_async_copy(hidden_ref, hid, hid_sem)

    def own_load(g):
        return pltpu.make_async_copy(
            weight_ref.at[:, pl.ds(pl.multiple_of(g * LANES, LANES), LANES)],
            wbuf.at[g, s], own_sem.at[g],
        )

    own_load(0).start()
    own_load(1).start()
    mats = (
        pltpu.make_async_copy(down_ref, downs.at[:, h], mat_sem.at[0]),
        pltpu.make_async_copy(up_ref, ups.at[h], mat_sem.at[1]),
    )

    barrier = pltpu.get_barrier_semaphore()
    for j in range(1, H):
        pl.semaphore_signal(barrier, inc=1, device_id=(s, (h + j) % H), device_id_type=MESH)
    for j in range(1, A):
        pl.semaphore_signal(
            barrier, inc=1, device_id=((a + j) % A * B + b, h), device_id_type=MESH
        )
    for j in range(1, B):
        pl.semaphore_signal(
            barrier, inc=1, device_id=(a * B + (b + j) % B, h), device_id_type=MESH
        )
    load.start()
    for g in range(2, G):
        own_load(g).start()
    for m in mats:
        m.start()
    pl.semaphore_wait(barrier, H - 1 + A - 1 + B - 1)

    def remote(src, dst, ssem, rsem, peer):
        return pltpu.make_async_remote_copy(
            src_ref=src, dst_ref=dst, send_sem=ssem, recv_sem=rsem,
            device_id=peer, device_id_type=MESH,
        )

    ways = (
        (a + 1 < A, s + B),
        (a > 0, s - B),
        (b + 1 < B, s + 1),
        (b > 0, s - 1),
    )

    def part(way, peer, g, o, lo, hi, rsem):
        block = wbuf.at[g, o, pl.ds(lo, hi - lo)]
        return remote(block, block, send_sem.at[way, g, o], rsem, (peer, h))

    def forwards(da, db, g, o, i):
        first = bounds[i] >= late
        conds = (
            (da >= 0) & (first | (db == 0)),
            (da <= 0) & (first | (db == 0)),
            (db >= 0) & ((not first) | (da == 0)),
            (db <= 0) & ((not first) | (da == 0)),
        )
        for way in range(4):
            @pl.when(ways[way][0] & conds[way])
            def _():
                part(
                    way, ways[way][1], g, o, bounds[i], bounds[i + 1], recv_sem.at[g, o, i]
                ).start()

    def own_start(g):
        own_load(g).wait()
        for i in range(pieces):
            forwards(0, 0, g, s, i)

    own_start(0)
    own_start(1)

    def to_head(m, hh):
        if m == 0:
            return remote(down_ref, downs.at[:, h], m_send.at[0, hh], m_recv.at[0, h], (s, hh))
        return remote(up_ref, ups.at[h], m_send.at[1, hh], m_recv.at[1, h], (s, hh))

    def from_head(m, hh):
        if m == 0:
            return remote(down_ref, downs.at[:, hh], m_send.at[0, hh], m_recv.at[0, hh], (s, hh))
        return remote(up_ref, ups.at[hh], m_send.at[1, hh], m_recv.at[1, hh], (s, hh))

    for m in range(2):
        for j in range(1, H):
            to_head(m, (h + j) % H).start()

    lane = lax.broadcasted_iota(jnp.int32, (LANES, LANES), 1)
    low = lane < HEAD_SIZE // 2
    sign = jnp.where(low, -1.0, 1.0)
    pos = pos_ref[...].astype(F32)
    blocks = rows // LANES
    for i in range(blocks // 2):
        k = i + blocks // 2
        p1 = jnp.broadcast_to(pos[i : i + 1], (LANES, LANES)).T
        p2 = jnp.broadcast_to(pos[k : k + 1], (LANES, LANES)).T
        angle = jnp.where(low, p1, p2) * freq_ref[...]
        ca, sa = jnp.cos(angle), jnp.sin(angle)
        cr, sr = pltpu.roll(ca, HEAD_SIZE // 2, 1), pltpu.roll(sa, HEAD_SIZE // 2, 1)
        r1, r2 = slice(i * LANES, (i + 1) * LANES), slice(k * LANES, (k + 1) * LANES)
        cosine[r1] = jnp.where(low, ca, cr)
        cosine[r2] = jnp.where(low, cr, ca)
        sine[r1] = jnp.where(low, sa, sr) * sign
        sine[r2] = jnp.where(low, sr, sa) * sign
    esum[...] = jnp.zeros_like(esum)
    msum[...] = jnp.zeros_like(msum)
    lat_acc[...] = jnp.zeros_like(lat_acc)
    acc[...] = jnp.zeros_like(acc)
    load.wait()

    def product(g, o, q):
        lo, span = spans[q], spans[q + 1] - spans[q]
        start = pl.multiple_of(o * depth + lo, min(span, 256))
        w = wbuf[g, o, lo : lo + span]
        step = 512
        for m in range(0, rows, step):
            acc[g, m : m + step] += jnp.dot(
                hid[m : m + step, pl.ds(start, span)], w, preferred_element_type=F32
            )

    def to_peer(g, r, hh):
        return remote(
            own_t.at[g, hh % 2, r], all_t.at[g, h, r], x_send.at[g, r, hh], x_recv.at[g, r, h],
            (s, hh),
        )

    def from_peer(g, r, hh):
        return remote(
            own_t.at[g, core, r], all_t.at[g, hh, r], x_send.at[g, r, hh], x_recv.at[g, r, hh],
            (s, hh),
        )

    def finish(g):
        is_key = (g % 2) == 0
        for r in range(tiles):
            for c in range(2):
                lo = (c * tiles + r) * tile

                @pl.when(is_key)
                def _():
                    key = acc[g, lo : lo + tile]
                    turned = key * cosine[lo : lo + tile] + pltpu.roll(
                        key, HEAD_SIZE // 2, 1
                    ) * sine[lo : lo + tile]
                    own_t[g, c, r] = turned.astype(BF16)

                @pl.when(jnp.logical_not(is_key))
                def _():
                    own_t[g, c, r] = acc[g, lo : lo + tile].astype(BF16)
            for j in range(1, H):
                to_peer(g, r, (h + j) % H).start()
            all_t[g, h, r] = own_t[g, core, r]

    def latent(g, r):
        for j in range(1, H):
            from_peer(g, r, (h + j) % H).wait_recv()
        x = jnp.concatenate([all_t[g, hh, r] for hh in range(H)], axis=1)
        d = downs[g].reshape(H * LANES, rank)
        lat_acc[r] += jnp.dot(x, d, preferred_element_type=F32)
        wide = x.astype(F32)
        esum[...] += jnp.sum((wide * wide).reshape(tile // 8, 8, H * LANES), axis=0)

    combos = 2 * (2 * B - 1)

    def combo(u, t):
        m = t // 2
        e = (m + 1) // 2
        off = e if m % 2 == 1 else -e
        side = 1 - 2 * (t % 2)
        d = u + 1 - e
        a0, b0 = a + side * d, b + off
        ok = (d >= 0) & (a0 >= 0) & (a0 < A) & (b0 >= 0) & (b0 < B)
        ok = ok & ((d > 0) | (side > 0))
        return ok, a - a0, b - b0, a0 * B + b0

    last_stage = A + B - 3

    def begin(g):
        for q in range(pieces):
            product(g, s, q)

    begin(0)
    begin(1)

    def arrivals(g, u):
        for i in range(pieces):
            def arrive(t, carry):
                ok, da, db, o = combo(u, t)

                @pl.when(ok)
                def _():
                    part(
                        0, s, g, o, bounds[i], bounds[i + 1], recv_sem.at[g, o, i]
                    ).wait_recv()
                    forwards(da, db, g, o, i)
                return carry
            [arrive(t, 0) for t in range(combos)]

            def multiply(t, carry):
                ok, _, _, o = combo(u, t)

                @pl.when(ok)
                def _():
                    product(g, o, i)
                return carry
            [multiply(t, 0) for t in range(combos)]

    def step(tau, carry):
        def group(g, carry):
            u = tau - g

            @pl.when((u >= 0) & (u <= last_stage))
            def _():
                arrivals(g, u)

            @pl.when((u == last_stage) & (g < G - 1))
            def _():
                finish(g)

            @pl.when((u == last_stage) & (g == 0))
            def _():
                mats[0].wait()
                for j in range(1, H):
                    from_head(0, (h + j) % H).wait_recv()

            @pl.when((u == last_stage) & (g > 0) & (g < G - 1))
            def _():
                for r in range(tiles):
                    latent(jnp.maximum(g - 1, 0), r)

            @pl.when(u == -2)
            def _():
                own_start(g)
                begin(g)
            return carry
        return lax.fori_loop(0, G, group, carry)
    lax.fori_loop(0, last_stage + G, step, 0)

    def nt(x, w):
        return lax.dot_general(x, w, (((1,), (1,)), ((), ())), preferred_element_type=F32)

    def tn(x, w):
        return lax.dot_general(x, w, (((0,), (0,)), ((), ())), preferred_element_type=F32)

    def to_sib(k, r, c):
        buf = (lat, dlat)[k].at[c, r]
        return remote(buf, buf, l_send.at[k, r], l_recv.at[k, r], (s, sib))

    last = G - 1
    finish(last)
    for r in range(tiles):
        latent(last - 1, r)
    mats[1].wait()
    for j in range(1, H):
        from_head(1, (h + j) % H).wait_recv()

    def columns(ref, *at):
        return jnp.concatenate([ref[(g,) + at] for g in range(G)], axis=1)

    for r in range(tiles):
        latent(last, r)
        narrow = lat_acc[r].astype(BF16)
        lat[core, r] = narrow
        to_sib(0, r, core).start()
        for hh in range(H):
            left = columns(all_t, hh, r).astype(F32) - jnp.dot(
                narrow, ups[hh], preferred_element_type=F32
            )
            res[hh, r] = left.astype(BF16)
            msum[...] += jnp.sum((left * left).reshape(tile // 8, 8, cols), axis=0)

    small = e0.shape[-2:]
    e0[core, 0] = jnp.full(small, jnp.sum(esum[...]), F32)
    e0[core, 1] = jnp.full(small, jnp.sum(msum[...]), F32)

    def level0(c):
        return remote(e0.at[c], e0.at[c], e_send.at[0], e0_recv, (s, sib))

    def level1(bb, slot):
        return remote(e1.at[slot], e1.at[slot], e_send.at[1 + bb], e1_recv.at[slot], (a * B + bb, h))

    def level2(aa, slot):
        return remote(
            e2.at[slot], e2.at[slot], e_send.at[1 + B + aa], e2_recv.at[slot], (aa * B + b, h)
        )

    level0(core).start()

    def first_hop(k, aa, bb, slot):
        return remote(
            gs1.at[k, aa, bb], gr1.at[k, aa, slot], g1_send.at[k, aa, bb], g1_recv.at[k, aa, slot],
            (a * B + bb, h),
        )

    def second_hop(k, aa, slot):
        return remote(
            gs2.at[k, aa], gr2.at[k, slot], g2_send.at[k, aa], g2_recv.at[k, slot],
            (aa * B + b, h),
        )

    def scatter(k, value):
        value = value.reshape(grad.shape[1:])
        grad[k] = value
        gs1[k] = value.astype(BF16)
        for i in range(1, A + 1):
            for j in range(1, B):
                first_hop(k, (a + i) % A, (b + j) % B, b).start()

    def combine(k):
        for i in range(1, A + 1):
            aa = (a + i) % A
            total = grad[k, aa, b]
            for j in range(1, B):
                bb = (b + j) % B
                first_hop(k, aa, bb, bb).wait_recv()
                total += gr1[k, aa, bb].astype(F32)
            if i < A:
                gs2[k, aa] = total.astype(BF16)
                second_hop(k, aa, a).start()
            else:
                fin[k] = total

    for r in range(tiles):
        to_sib(0, r, other).wait_recv()
        left = columns(own_t, other, r).astype(F32) - jnp.dot(
            lat[other, r], ups[h], preferred_element_type=F32
        )
        res_o[r] = left.astype(BF16)
    half = tiles * tile
    scatter(
        0,
        tn(lat[core].reshape(half, rank), res[h].reshape(half, cols))
        + tn(lat[other].reshape(half, rank), res_o[...].reshape(half, cols)),
    )

    for r in range(tiles):
        total = nt(res[0, r], ups[0])
        for hh in range(1, H):
            total += nt(res[hh, r], ups[hh])
        dlat[core, r] = total.astype(BF16)
        to_sib(1, r, core).start()

    level0(other).wait_recv()
    e1[b] = e0[0] + e0[1]
    for j in range(1, B):
        level1((b + j) % B, b).start()

    def targets(c):
        return jnp.concatenate(
            [own_t[g, c].reshape(half, LANES) for g in range(G)], axis=1
        )

    mine = tn(dlat[core].reshape(half, rank), targets(core))
    for r in range(tiles):
        to_sib(1, r, other).wait_recv()
    scatter(1, mine + tn(dlat[other].reshape(half, rank), targets(other)))

    total = None
    for j in range(1, B):
        bb = (b + j) % B
        level1(bb, bb).wait_recv()
    total = e1[0]
    for bb in range(1, B):
        total += e1[bb]
    e2[a] = total
    for j in range(1, A):
        level2((a + j) % A, a).start()

    combine(0)
    combine(1)

    def sends(n, carry):
        g, o = n // N, n % N
        da, db = a - o // B, b - o % B
        zs = (da >= 0, da <= 0)
        xs = (db >= 0, db <= 0)
        for way in range(2):
            @pl.when(ways[way][0] & zs[way] & (db == 0))
            def _():
                part(way, s, g, o, 0, depth, recv_sem.at[g, o, 0]).wait_send()
            if late < depth:
                @pl.when(ways[way][0] & zs[way] & (db != 0))
                def _():
                    part(way, s, g, o, late, depth, recv_sem.at[g, o, 0]).wait_send()
        for way in range(2, 4):
            @pl.when(ways[way][0] & xs[way - 2] & (da == 0))
            def _():
                part(way, s, g, o, 0, depth, recv_sem.at[g, o, 0]).wait_send()

            @pl.when(ways[way][0] & xs[way - 2] & (da != 0))
            def _():
                part(way, s, g, o, 0, late, recv_sem.at[g, o, 0]).wait_send()
        return carry
    lax.fori_loop(0, G * N, sends, 0)
    for j in range(1, H):
        hh = (h + j) % H
        for m in range(2):
            to_head(m, hh).wait_send()
        for r in range(tiles):
            for g in range(G):
                to_peer(g, r, hh).wait_send()
    for k in range(2):
        for r in range(tiles):
            to_sib(k, r, core).wait_send()
        for i in range(1, A + 1):
            for j in range(1, B):
                first_hop(k, (a + i) % A, (b + j) % B, b).wait_send()
    level0(core).wait_send()
    for j in range(1, B):
        level1((b + j) % B, b).wait_send()

    for j in range(1, A):
        aa = (a + j) % A
        level2(aa, aa).wait_recv()
    total = e2[0]
    for aa in range(1, A):
        total += e2[aa]
    whole_energy, whole_misfit = total[0], total[1]
    rel_ref[...] = whole_misfit / whole_energy
    factor = (-(entry_items / whole_energy) / math.sqrt(token_count))[0:1, 0:1]

    for k, out in ((0, gu_ref), (1, gd_ref)):
        total = fin[k]
        for i in range(1, A):
            aa = (a + i) % A
            second_hop(k, aa, aa).wait_recv()
            total += gr2[k, aa].astype(F32)
        out[...] = factor * total
    for k in range(2):
        for i in range(1, A):
            second_hop(k, (a + i) % A, a).wait_send()
    for j in range(1, A):
        level2((a + j) % A, a).wait_send()


def fused(N, H, freqs, positions, hidden, weight, down, up):
    B = 2 if N <= 8 else 8
    A = N // B
    rows, width = hidden.shape
    depth, cols = weight.shape
    rank = down.shape[1]
    G = cols // LANES
    block = rank // N
    tiles = 2
    tile = rows // 2 // tiles
    bounds, late = cut(depth, B)
    pieces = len(bounds) - 1
    token_count = N * rows
    dma = pltpu.SemaphoreType.DMA
    vmem = pl.BlockSpec(memory_space=pltpu.VMEM)
    hbm = pl.BlockSpec(memory_space=pltpu.HBM)
    return pl.pallas_call(
        functools.partial(
            kernel, A, B, H, bounds, late,
            token_count * 2 * KEY_VALUE_HEADS * HEAD_SIZE, token_count,
        ),
        out_shape=(
            jax.ShapeDtypeStruct((block, cols), F32),
            jax.ShapeDtypeStruct((block, cols), F32),
            jax.ShapeDtypeStruct((8, LANES), F32),
        ),
        in_specs=[vmem] * 2 + [hbm] * 4,
        out_specs=(vmem,) * 3,
        scratch_shapes=[
            pltpu.VMEM((rows, width), BF16),
            pltpu.VMEM((G, N, depth, LANES), BF16),
            pltpu.VMEM((G, rows, LANES), F32),
            pltpu.VMEM((rows, LANES), F32),
            pltpu.VMEM((rows, LANES), F32),
            pltpu.VMEM((G, 2, tiles, tile, LANES), BF16),
            pltpu.VMEM((G, H, tiles, tile, LANES), BF16),
            pltpu.VMEM((G, H, LANES, rank), BF16),
            pltpu.VMEM((H, rank, cols), BF16),
            pltpu.VMEM((tiles, tile, rank), F32),
            pltpu.VMEM((2, tiles, tile, rank), BF16),
            pltpu.VMEM((2, tiles, tile, rank), BF16),
            pltpu.VMEM((H, tiles, tile, cols), BF16),
            pltpu.VMEM((tiles, tile, cols), BF16),
            pltpu.VMEM((2, A, B, block, cols), F32),
            pltpu.VMEM((2, A, B, block, cols), BF16),
            pltpu.VMEM((2, A, B, block, cols), BF16),
            pltpu.VMEM((2, A, block, cols), BF16),
            pltpu.VMEM((2, A, block, cols), BF16),
            pltpu.VMEM((2, block, cols), F32),
            pltpu.VMEM((8, H * LANES), F32),
            pltpu.VMEM((8, cols), F32),
            pltpu.VMEM((2, 2, 8, LANES), F32),
            pltpu.VMEM((B, 2, 8, LANES), F32),
            pltpu.VMEM((A, 2, 8, LANES), F32),
            dma,
            dma((G,)),
            dma((2,)),
            dma((4, G, N)),
            dma((G, N, pieces)),
            dma((2, H)),
            dma((2, H)),
            dma((G, tiles, H)),
            dma((G, tiles, H)),
            dma((2, tiles)),
            dma((2, tiles)),
            dma((2, A, B)),
            dma((2, A, B)),
            dma((2, A)),
            dma((2, A)),
            dma((1 + A + B,)),
            dma,
            dma((B,)),
            dma((A,)),
        ],
        compiler_params=pltpu.CompilerParams(
            collective_id=0, has_side_effects=True, vmem_limit_bytes=54912 * 2**10
        ),
    )(
        freqs, positions.reshape(rows // LANES, LANES), hidden, weight,
        down.reshape(G, LANES, rank), up,
    )


def solution(mesh):
    N, H = mesh.shape["seq"], mesh.shape["head"]

    def per_device(hidden, key_value_weight, down_projection, up_projection, positions):
        grad_down, grad_up, rel = fused(
            N, H, frequencies(), positions, hidden, key_value_weight, down_projection, up_projection
        )
        return grad_down, grad_up, rel[0, 0]

    return jax.shard_map(
        per_device,
        mesh=mesh,
        in_specs=(P("seq", None), P("seq", "head"), P("head", None), P(None, "head"), P("seq")),
        out_specs=(P("seq", "head"), P("seq", "head"), P()),
        check_vma=False,
    )
```
